512 devices in a mesh: page: 64 (over x, z), head: 8 (over y, core).
Axes of the slice: x: 4, y: 4, z: 16, core: 2. Of those that a mesh axis runs over, the one named last changes fastest.
Arguments:
- hidden: bfloat16 [24576, 4096], P('page'), may hold values from -6 to 6
- attention_norm_gain: bfloat16 [4096], replicated, may hold values from 0.25 to 1.75
- wq: bfloat16 [4096, 4096], P('page', 'head'), may hold values from -0.09375 to 0.09375
- adapter_down_weight: bfloat16 [4096, 1024], P('head', 'page'), may hold values from -0.09375 to 0.09375
- adapter_up_weight: bfloat16 [1024, 4096], P('page', 'head'), may hold values from -0.75 to 0.75
- key_value_cache: bfloat16 [24576, 2, 1024], P('page', None, 'head'), may hold values from -110 to 110
- logical_page_table: int32 [64, 3], P('page'), may hold values from 0 to 2, each once within a row
- lengths: int32 [16], replicated, may hold values from 1 to 6144, 24576 in all
- prompt_adapter_index: int32 [16], replicated, may hold values from 0 to 63
Outputs:
- queries: bfloat16 [24576, 4096], P('page', 'head')
- attended: bfloat16 [24576, 4096], P('page', 'head')
The draws below stay inside these ranges and needn't reach their ends.
Inputs may be any that keep to these rules, and one draw needn't show every extreme that they name: The lengths sum to 24576 and the longest is exactly 6144. `logical_page_table`: each row is a permutation of the page slots of one index of page.
All inputs are finite; a program needn't handle non-finite values.
Results may differ from the reference program's by a relative error of at most 0.012.
The reference program's roundings to bfloat16 on the way count: a program that leaves them out, or rounds other values in their place, can miss the bound.
Values may be sent and summed in bfloat16 or wider, within the bound.
A program may use at most 128 MiB of HBM per device.

```python
import math
import jax
import jax.numpy as jnp
import numpy as np
from jax import lax

MODEL_WIDTH = 4096
QUERY_HEADS = 32
KVH = 8
HEAD_WIDTH = 128
ADAPTER_RANK = 16
TOK_DEV = 384
PAGE = 128
SPAN = 16
ADAPTER_TOTAL = 64
TOKEN_TOTAL = 24576
REQUESTS = 16
PAGES_DEV = 3
N_PAGE = 64


def draw_key_value_cache(key, part):
    first_key = jax.random.fold_in(key, 0)
    output_shape = (TOKEN_TOTAL, 2, KVH * HEAD_WIDTH)
    values = jnp.clip(jax.random.normal(first_key, output_shape, jnp.float32), -4.0, 4.0)
    return values.astype(jnp.bfloat16)


def touch_ends(array, stream_key, smallest, largest):
    longest = array.shape.index(max(array.shape))
    spots = []
    for shift in (0, 1):
        where = [jax.random.randint(jax.random.fold_in(stream_key, axis), (), 0, length) for axis, length in enumerate(array.shape)]
        where[longest] = (where[longest] + shift) % array.shape[longest]
        spots.append(tuple(where))
    return array.at[spots[0]].set(smallest).at[spots[1]].set(largest)


def levels(rng, shape, cuts, smallest, top_value):
    gain = 1.0
    for position, shards_of in cuts:
        heights = jax.random.uniform(jax.random.fold_in(jax.random.fold_in(rng, 6), position), (shards_of,), jnp.float32, smallest / len(cuts), top_value / len(cuts))
        gain = gain * jnp.repeat(jnp.exp(heights), shape[position] // shards_of).reshape((-1,) + (1,) * (len(shape) - 1 - position))
    return gain


def rank_table(amount, slope):
    weights = [(1 << 20) // math.isqrt(standing ** slope) + 1 for standing in range(1, amount + 1)]
    scale = 1 + sum(weights) // (1 << 30)
    return np.cumsum(np.array([max(1, weight // scale) for weight in weights]))


def ranked_ids(rng, extent, amount, slope):
    table = rank_table(amount, slope)
    lot = jax.random.randint(jax.random.fold_in(rng, 1), extent, 0, int(table[amount - 1]))
    grade = jnp.searchsorted(jnp.asarray(table, jnp.int32), lot, side="right")
    return jax.random.permutation(jax.random.fold_in(rng, 2), amount)[grade].astype(jnp.int32)


def profile(number_of, total, bound, slope):
    loads = [(1 << 20) // math.isqrt(grade ** slope) + 1 for grade in range(2, number_of + 1)]
    rest, given = total - bound - (number_of - 1), [1] * (number_of - 1)
    while rest > 0:
        free = [i for i in range(number_of - 1) if given[i] < bound]
        pool, left = sum([loads[i] for i in free]), rest
        for i in free:
            more = min(bound - given[i], max(1, left * loads[i] // pool), rest)
            given[i] = given[i] + more
            rest = rest - more
    return np.array([bound] + given)


def ragged(key, count, total, reach, slope):
    if count == 2:
        one = jax.random.randint(key, (), max(1, total - reach), min(reach, total - 1) + 1)
        return jnp.stack([one, total - one])
    tallies = jnp.asarray(profile(count, total, reach, slope), jnp.int32)
    pairs = (count - 1) // 2
    donor, receiver = tallies[1:1 + 2 * pairs:2], tallies[2:2 + 2 * pairs:2]
    slack = jnp.minimum(donor - 1, reach - receiver)
    passed = jax.random.randint(jax.random.fold_in(key, 1), (pairs,), 0, 1 << 20) % (slack + 1)
    tallies = tallies.at[1:1 + 2 * pairs:2].set(donor - passed).at[2:2 + 2 * pairs:2].set(receiver + passed)
    return tallies[jax.random.permutation(jax.random.fold_in(key, 2), count)]


def centred(stream_key, shape, spread, most, shards=(), held_as=jnp.bfloat16):
    array = spread * jax.random.normal(stream_key, shape, jnp.float32)
    if shards:
        array = array * levels(stream_key, shape, shards, -0.22, 0.18)
    return jnp.clip(array, -most, most).astype(held_as)


def setup_inputs(seed: int = 0) -> dict:
    seeds = jax.random.split(jax.random.key(seed), 10)
    return {
        "hidden": centred(seeds[0], (TOKEN_TOTAL, MODEL_WIDTH), 1.0, 6.0, ((0, 64),)),
        "attention_norm_gain": jnp.clip(1.0 + 0.15 * jax.random.normal(seeds[1], (MODEL_WIDTH,), jnp.float32), 0.25, 1.75).astype(jnp.bfloat16),
        "wq": centred(seeds[2], (MODEL_WIDTH, QUERY_HEADS * HEAD_WIDTH), MODEL_WIDTH ** -0.5, 0.09375, ((0, 64), (1, 8))),
        "adapter_down_weight": centred(seeds[3], (MODEL_WIDTH, ADAPTER_TOTAL * ADAPTER_RANK), MODEL_WIDTH ** -0.5, 0.09375, ((0, 8), (1, 64))),
        "adapter_up_weight": centred(seeds[4], (ADAPTER_TOTAL * ADAPTER_RANK, QUERY_HEADS * HEAD_WIDTH), (4 * ADAPTER_RANK) ** -0.5, 0.75, ((0, 64), (1, 8))),
        "key_value_cache": draw_key_value_cache(jax.random.fold_in(seeds[9], 71), 0),
        "logical_page_table": jax.vmap(lambda own: jax.random.permutation(own, PAGES_DEV))(jax.random.split(seeds[6], N_PAGE)).reshape((N_PAGE, PAGES_DEV)).astype(jnp.int32),
        "lengths": ragged(seeds[7], REQUESTS, TOKEN_TOTAL, SPAN * TOK_DEV, 2).astype(jnp.int32),
        "prompt_adapter_index": touch_ends(ranked_ids(seeds[8], (REQUESTS,), ADAPTER_TOTAL, 2), jax.random.fold_in(seeds[8], 3), 0, ADAPTER_TOTAL - 1).astype(jnp.int32),
    }


EPSILON = 1e-05
ROPE_BASE = 500000.0

def apply_rotation(values_f, token_position):
    half = HEAD_WIDTH // 2
    inverse = ROPE_BASE ** (-(jnp.arange(half, dtype=jnp.float32) * 2.0 / HEAD_WIDTH))
    angle = token_position.astype(jnp.float32)[:, None] * inverse[None, :]
    cosine = jnp.cos(angle)[:, None, :]
    sine = jnp.sin(angle)[:, None, :]
    first = values_f[..., :half]
    second = values_f[..., half:]
    return jnp.concatenate([first * cosine - second * sine, second * cosine + first * sine], axis=-1)

def reference(hidden, attention_norm_gain, wq, adapter_down_weight, adapter_up_weight, key_value_cache, logical_page_table, lengths, prompt_adapter_index):
    x = hidden.astype(jnp.float32)
    scale_rows = lax.rsqrt(lax.optimization_barrier(jnp.mean(x * x, axis=-1, keepdims=True)) + EPSILON)
    normed_input = (x * scale_rows * attention_norm_gain.astype(jnp.float32)).astype(jnp.bfloat16)
    ends = jnp.cumsum(lengths).astype(jnp.int32)
    starts = (ends - lengths).astype(jnp.int32)
    token = jnp.arange(TOKEN_TOTAL, dtype=jnp.int32)
    member = (token[:, None] >= starts[None, :]) & (token[:, None] < ends[None, :])
    tok_start = lax.optimization_barrier(jnp.sum(jnp.where(member, starts[None, :], 0), axis=1)).astype(jnp.int32)
    tok_adapter = lax.optimization_barrier(jnp.sum(jnp.where(member, prompt_adapter_index[None, :], 0), axis=1)).astype(jnp.int32)
    token_position = token - tok_start
    base_query = jnp.dot(normed_input, wq, preferred_element_type=jnp.float32)
    partial_every_token = jnp.dot(normed_input, adapter_down_weight, preferred_element_type=jnp.float32).reshape(TOKEN_TOTAL, ADAPTER_TOTAL, ADAPTER_RANK)
    pick = tok_adapter[:, None] == jnp.arange(ADAPTER_TOTAL, dtype=jnp.int32)[None, :]
    shrunk = lax.optimization_barrier(jnp.sum(jnp.where(pick[:, :, None], partial_every_token, 0.0), axis=1)).astype(jnp.bfloat16)
    spread_heads = jnp.where(pick[:, :, None], shrunk[:, None, :], jnp.zeros((), jnp.bfloat16)).reshape(TOKEN_TOTAL, ADAPTER_TOTAL * ADAPTER_RANK)
    adapter_delta = jnp.dot(spread_heads, adapter_up_weight, preferred_element_type=jnp.float32)
    queries = apply_rotation((base_query + adapter_delta).reshape(TOKEN_TOTAL, QUERY_HEADS, HEAD_WIDTH), token_position).astype(jnp.bfloat16)
    paged = key_value_cache.reshape(N_PAGE, PAGES_DEV, PAGE, 2, KVH * HEAD_WIDTH)
    ordered = jax.vmap(lambda blocks, table: jnp.take(blocks, table, axis=0))(paged, logical_page_table)
    ordered = ordered.reshape(TOKEN_TOTAL, 2, KVH, HEAD_WIDTH)
    margin = SPAN * TOK_DEV
    padded = jnp.concatenate([jnp.zeros((margin, 2, KVH, HEAD_WIDTH), ordered.dtype), ordered], axis=0)
    inv_scale = 1.0 / math.sqrt(HEAD_WIDTH)

    def one_block(index):
        first = (index * TOK_DEV).astype(jnp.int32)
        query_block = lax.dynamic_slice_in_dim(queries, first, TOK_DEV, 0).astype(jnp.float32)
        query_block = query_block.reshape(TOK_DEV, KVH, QUERY_HEADS // KVH, HEAD_WIDTH)
        window = lax.dynamic_slice_in_dim(padded, first, margin + TOK_DEV, 0).astype(jnp.float32)
        query_start = lax.dynamic_slice_in_dim(tok_start, first, TOK_DEV, 0)
        query_index = first + jnp.arange(TOK_DEV, dtype=jnp.int32)
        key_index = first - margin + jnp.arange(margin + TOK_DEV, dtype=jnp.int32)
        visible = (key_index[None, :] >= query_start[:, None]) & (key_index[None, :] <= query_index[:, None])
        scores = jnp.einsum('tkgd,skd->kgts', query_block, window[:, 0]) * inv_scale
        scores = jnp.where(visible[None, None], scores, -jnp.inf)
        top = lax.optimization_barrier(jnp.max(scores, axis=-1, keepdims=True))
        expo = jnp.exp(scores - top)
        weights = (expo / lax.optimization_barrier(jnp.sum(expo, axis=-1, keepdims=True))).astype(jnp.bfloat16)
        mixed = jnp.einsum('kgts,skd->tkgd', weights.astype(jnp.float32), window[:, 1])
        return mixed.reshape(TOK_DEV, QUERY_HEADS * HEAD_WIDTH).astype(jnp.bfloat16)
    attended = lax.map(one_block, jnp.arange(N_PAGE, dtype=jnp.int32)).reshape(TOKEN_TOTAL, QUERY_HEADS * HEAD_WIDTH)
    return (queries.reshape(TOKEN_TOTAL, QUERY_HEADS * HEAD_WIDTH), attended)
```

```python
import functools
import math

import jax
import jax.numpy as jnp
from jax import lax
from jax.experimental import pallas as pl
from jax.experimental.pallas import tpu as pltpu
from jax.sharding import PartitionSpec as P

HEAD_WIDTH = 128
RANK = 16
EPSILON = 1e-05
ROPE_BASE = 500000.0
NX = 4
MASKED = -1e30
LAG_NEAR = 2
LAG_FAR = 4


def clamp(value, low, high):
    return jnp.minimum(jnp.maximum(value, low), high)


def kernel(
    nz,
    nh,
    length_ref,
    prompt_adapter_ref,
    table_ref,
    hidden_ref,
    gain_ref,
    wq_ref,
    down_ref,
    up_ref,
    kv_ref,
    freq_ref,
    query_ref,
    out_ref,
    normed,
    own_feat,
    ga,
    gw,
    kvb,
    acc,
    start_col,
    adapter_col,
    adapter_row,
    cosine,
    sine,
    partial,
    psum,
    scores,
    recv_a,
    recv_w,
    send_za,
    send_zw,
    send_xa,
    send_xw,
    recv_kv,
    send_kf,
    send_kb,
    recv_h,
    send_h,
):
    page_axis = NX * nz
    tokens, width = hidden_ref.shape
    feat = wq_ref.shape[0]
    cols = wq_ref.shape[1]
    heads = cols // HEAD_WIDTH
    own_width = own_feat.shape[1]
    requests = length_ref.shape[0]
    pages = kv_ref.shape[0]
    page_rows = kv_ref.shape[1]
    me = lax.axis_index("page")
    head = lax.axis_index("head")
    x = me // nz
    z = me % nz
    z_up = x * nz + (z + 1) % nz
    z_down = x * nz + (z + nz - 1) % nz
    x_up = ((x + 1) % NX) * nz + z
    x_down = ((x + NX - 1) % NX) * nz + z
    p_up = (me + 1) % page_axis
    p_down = (me + page_axis - 1) % page_axis
    left_x = (x + NX - 1) % NX
    right_x = (x + 1) % NX
    far_x = (x + 2) % NX

    def send(src, dst, send_sem, recv_sem, page):
        return pltpu.make_async_remote_copy(
            src_ref=src,
            dst_ref=dst,
            send_sem=send_sem,
            recv_sem=recv_sem,
            device_id={"page": page},
            device_id_type=pl.DeviceIdType.MESH,
        )

    barrier = pltpu.get_barrier_semaphore()
    for page in (z_up, z_down, x_up, x_down, p_up, p_down):
        pl.semaphore_signal(
            barrier, inc=1, device_id={"page": page}, device_id_type=pl.DeviceIdType.MESH
        )
    for step in range(1, nh):
        pl.semaphore_signal(
            barrier,
            inc=1,
            device_id={"head": (head + step) % nh},
            device_id_type=pl.DeviceIdType.MESH,
        )

    ga[z, x, 0:RANK, :] = up_ref[...]
    ga[z, x, RANK : 2 * RANK, :] = (
        jnp.transpose(down_ref[...].astype(jnp.float32)).astype(jnp.bfloat16)
    )
    gw[z, x] = wq_ref[...]
    for j in range(pages):
        page_block = kv_ref[table_ref[0, j]]
        kvb[0, 0, j * page_rows : (j + 1) * page_rows, :] = page_block[:, :HEAD_WIDTH]
        kvb[0, 1, j * page_rows : (j + 1) * page_rows, :] = page_block[:, HEAD_WIDTH:]
    pl.semaphore_wait(barrier, 6 + nh - 1)

    low = nz // 4
    high = nz - 1 - low

    def reach(offset):
        return clamp(nz - 1 - (z + 2 * nz - offset) % nz, low, high)

    def kv_forward(offset, half):
        return send(
            kvb.at[offset, half],
            kvb.at[offset + 1, half],
            send_kf.at[offset, half],
            recv_kv.at[offset + 1, half],
            p_up,
        )

    def kv_backward(offset, half):
        return send(
            kvb.at[offset, half],
            kvb.at[offset - 1, half],
            send_kb.at[offset, half],
            recv_kv.at[offset - 1, half],
            p_down,
        )

    def kv_cross(half):
        return send(
            kvb.at[0, half],
            kvb.at[nz, half],
            send_kb.at[0, half],
            recv_kv.at[nz, half],
            x_up,
        )

    def kv_wait(offset, half):
        send(
            kvb.at[0, half],
            kvb.at[offset, half],
            send_kb.at[0, half],
            recv_kv.at[offset, half],
            x_up,
        ).wait_recv()

    def kv_step(j):
        reach_up = reach(j)
        back = nz + 1 - j
        reach_back = reach(back)
        for half in range(2):

            @pl.when(j <= reach_up)
            def _():
                kv_wait(j, half)

                @pl.when(j + 1 <= reach_up)
                def _():
                    kv_forward(j, half).start()

            @pl.when(back > reach_back)
            def _():
                kv_wait(back, half)

                @pl.when(back - 1 > reach_back)
                def _():
                    kv_backward(back, half).start()

    def position(i):
        distance = (i + 1) // 2
        return jnp.where(i % 2 == 1, (z + nz - distance) % nz, (z + distance) % nz)

    def weight_stream(buf, recv, send_z, send_x):
        def z_copy(i, zz, page, slot):
            return send(buf.at[zz, x], buf.at[zz, x], send_z.at[slot], recv.at[zz, x], page)

        def x_copy(zz, xx, page, which):
            return send(
                buf.at[zz, xx], buf.at[zz, xx], send_x.at[which, zz], recv.at[zz, xx], page
            )

        def wait(zz, xx):
            send(
                buf.at[zz, xx], buf.at[zz, xx], send_x.at[0, zz], recv.at[zz, xx], x_up
            ).wait_recv()

        def arrive(i):
            zz = position(i)

            @pl.when(i > 0)
            def _():
                wait(zz, x)

            @pl.when(((i % 2 == 1) & ((i + 1) // 2 < nz // 2)) | (i == 0))
            def _():
                z_copy(i, zz, z_up, i).start()

            @pl.when(((i % 2 == 0) & ((i + 1) // 2 < nz // 2 - 1)))
            def _():
                z_copy(i, zz, z_down, jnp.where(i == 0, nz, i)).start()

            x_copy(zz, x, x_up, 0).start()
            x_copy(zz, x, x_down, 1).start()

        def near(i):
            zz = position(i)
            wait(zz, left_x)

            @pl.when(i % 2 == 0)
            def _():
                x_copy(zz, left_x, x_up, 2).start()

            wait(zz, right_x)

            @pl.when(i % 2 == 1)
            def _():
                x_copy(zz, right_x, x_down, 2).start()

        def far(i):
            zz = position(i)
            wait(zz, far_x)
            return zz

        def finish(i):
            zz = position(i)

            @pl.when(((i % 2 == 1) & ((i + 1) // 2 < nz // 2)) | (i == 0))
            def _():
                z_copy(i, zz, z_up, i).wait_send()

            @pl.when(((i % 2 == 0) & ((i + 1) // 2 < nz // 2 - 1)))
            def _():
                z_copy(i, zz, z_down, jnp.where(i == 0, nz, i)).wait_send()

            x_copy(zz, x, x_up, 0).wait_send()
            x_copy(zz, x, x_down, 1).wait_send()
            x_copy(zz, left_x, x_up, 2).wait_send()

        return arrive, near, far, finish

    a_arrive, a_near, a_far, a_finish = weight_stream(ga, recv_a, send_za, send_xa)
    w_arrive, w_near, w_far, w_finish = weight_stream(gw, recv_w, send_zw, send_xw)

    a_arrive(0)
    for half in range(2):

        @pl.when(reach(0) >= 1)
        def _():
            kv_forward(0, half).start()

        kv_cross(half).start()

    def prompts(token):
        start = jnp.zeros(token.shape, jnp.int32)
        adapter = jnp.zeros(token.shape, jnp.int32)
        end = jnp.int32(0)
        for r in range(requests):
            begin = end
            end = end + length_ref[r]
            inside = (token >= begin) & (token < end)
            start = jnp.where(inside, begin, start)
            adapter = jnp.where(inside, prompt_adapter_ref[r], adapter)
        return start, adapter

    token_row = me * tokens + lax.broadcasted_iota(jnp.int32, (8, tokens), 1)
    adapter_row[...] = prompts(token_row)[1]

    rows_step = 32

    def norm_rows(step, carry):
        rows = pl.ds(pl.multiple_of(step * rows_step, rows_step), rows_step)
        value = hidden_ref[rows, :].astype(jnp.float32)
        scale = lax.rsqrt(jnp.mean(value * value, axis=-1, keepdims=True) + EPSILON)
        value = value * scale * gain_ref[...].astype(jnp.float32)
        lane = lax.broadcasted_iota(jnp.int32, (rows_step, 2 * feat), 1)
        lower = lane < feat
        for pair in range(nz // 2):
            piece = [
                value[:, (k * nz // 2 + pair) * 2 * feat : (k * nz // 2 + pair + 1) * 2 * feat]
                for k in range(NX)
            ]
            for k in range(0, NX, 2):
                even = jnp.where(lower, piece[k], pltpu.roll(piece[k + 1], feat, 1))
                odd = jnp.where(lower, pltpu.roll(piece[k], feat, 1), piece[k + 1])
                normed[2 * pair, rows, k * feat : (k + 2) * feat] = even.astype(jnp.bfloat16)
                normed[2 * pair + 1, rows, k * feat : (k + 2) * feat] = odd.astype(jnp.bfloat16)
        mine = pl.ds(pl.multiple_of(head * own_width, own_width), own_width)
        own = hidden_ref[rows, mine].astype(jnp.float32)
        own = own * scale * gain_ref[:, mine].astype(jnp.float32)
        own_feat[rows, :] = own.astype(jnp.bfloat16)
        token = me * tokens + step * rows_step + lax.broadcasted_iota(
            jnp.int32, (rows_step, HEAD_WIDTH), 0
        )
        start, adapter = prompts(token)
        start_col[rows, :] = start
        adapter_col[rows, :] = adapter
        return carry

    lax.fori_loop(0, tokens // rows_step, norm_rows, 0)
    acc[...] = jnp.zeros_like(acc)
    partial[...] = jnp.zeros_like(partial)

    def head_copy(step):
        return pltpu.make_async_remote_copy(
            src_ref=psum.at[0],
            dst_ref=psum.at[step],
            send_sem=send_h.at[step],
            recv_sem=recv_h.at[step],
            device_id={"head": (head + step) % nh},
            device_id_type=pl.DeviceIdType.MESH,
        )

    def stage(n, first, count, body):
        @pl.when((n >= first) & (n < first + count))
        def _():
            body(n - first)

    def a_compute(i):
        zz = a_far(i)
        block = ga[zz, :, RANK : 2 * RANK, :].reshape(NX * RANK, cols)
        part = lax.dot_general(
            block, own_feat[...], (((1,), (1,)), ((), ())), preferred_element_type=jnp.float32
        )
        wanted = adapter_row[...]
        wanted = jnp.concatenate([wanted, wanted], axis=0)
        total = partial[...]
        for k in range(NX):
            total += jnp.where(wanted == k * nz + zz, part[k * RANK : (k + 1) * RANK], 0.0)
        partial[...] = total

        @pl.when(i == nz - 1)
        def _():
            psum[0] = total
            for step in range(1, nh):
                head_copy(step).start()

    def w_compute(i):
        zz = w_far(i)
        acc[...] += jnp.dot(
            normed[zz], gw[zz].reshape(NX * feat, cols), preferred_element_type=jnp.float32
        )

    early = nz // 4

    def weights_step(n, carry):
        stage(n, 1, nz - 1, lambda i: a_arrive(i + 1))
        stage(n, nz, nz, w_arrive)
        stage(n, LAG_NEAR, nz, a_near)
        stage(n, nz + LAG_NEAR, nz, w_near)
        stage(n, LAG_FAR, nz, a_compute)

        @pl.when((n < nz) & (n % 4 == 3))
        def _():
            kv_step((n + 1) // 4)

        stage(n, nz + LAG_FAR, nz, w_compute)

        @pl.when((n >= nz) & (n < 2 * nz) & ((n - nz) % 2 == 1))
        def _():
            kv_step(early + (n - nz + 1) // 2)

        return carry

    lax.fori_loop(0, 2 * nz + LAG_FAR, weights_step, 0)

    def late_step(j, carry):
        kv_step(j)
        return carry

    for step in range(1, nh):
        head_copy(step).wait_recv()
    shrunk = psum[0]
    for step in range(1, nh):
        shrunk = shrunk + psum[step]
    shrunk = shrunk.astype(jnp.bfloat16).astype(jnp.float32)
    shrunk = jnp.concatenate([shrunk] * (HEAD_WIDTH // RANK), axis=0)
    shrunk = jnp.transpose(shrunk)
    lane = lax.broadcasted_iota(jnp.int32, (tokens, HEAD_WIDTH), 1)
    per = HEAD_WIDTH // RANK
    spread = []
    for c in range(page_axis // per):
        group = c * per + lane // RANK
        adapter = (group % NX) * nz + group // NX
        spread.append(jnp.where(adapter_col[...] == adapter, shrunk, 0.0).astype(jnp.bfloat16))
    spread = jnp.concatenate(spread, axis=1)
    delta = jnp.dot(
        spread,
        ga[:, :, 0:RANK, :].reshape(page_axis * RANK, cols),
        preferred_element_type=jnp.float32,
    )
    acc[...] += delta

    token = me * tokens + lax.broadcasted_iota(jnp.int32, (tokens, HEAD_WIDTH), 0)
    angle = (token - start_col[...]).astype(jnp.float32) * freq_ref[...]
    cosine[...] = jnp.cos(angle)
    sine[...] = jnp.where(lane < HEAD_WIDTH // 2, -jnp.sin(angle), jnp.sin(angle))
    for h in range(heads):
        u = acc[:, h * HEAD_WIDTH : (h + 1) * HEAD_WIDTH]
        turned = u * cosine[...] + pltpu.roll(u, HEAD_WIDTH // 2, 1) * sine[...]
        query_ref[:, h * HEAD_WIDTH : (h + 1) * HEAD_WIDTH] = turned.astype(jnp.bfloat16)

    lax.fori_loop(early + nz // 2 + 1, nz + 1, late_step, 0)

    factor = math.log2(math.e) / math.sqrt(HEAD_WIDTH)
    lane = lax.broadcasted_iota(jnp.int32, (tokens, HEAD_WIDTH), 1)
    begin = start_col[...] - lane
    row = lax.broadcasted_iota(jnp.int32, (tokens, HEAD_WIDTH), 0)
    pieces = tokens // HEAD_WIDTH

    def attend(h, carry):
        where_h = pl.ds(pl.multiple_of(h * HEAD_WIDTH, HEAD_WIDTH), HEAD_WIDTH)
        query = query_ref[:, where_h]

        def score(offset, top, causal):
            block = lax.dot_general(
                query,
                kvb[offset, 0],
                (((1,), (1,)), ((), ())),
                preferred_element_type=jnp.float32,
            )
            base = (me - offset) * tokens
            for c in range(pieces):
                visible = begin <= base + c * HEAD_WIDTH
                if causal:
                    visible = visible & (lane + c * HEAD_WIDTH <= row)
                part = block[:, c * HEAD_WIDTH : (c + 1) * HEAD_WIDTH]
                part = jnp.where(visible, part, MASKED)
                scores[offset, :, c * HEAD_WIDTH : (c + 1) * HEAD_WIDTH] = part
                top = part if top is None else jnp.maximum(top, part)
            return top

        top = score(0, None, True)
        top = lax.fori_loop(1, nz + 1, lambda o, t: score(o, t, False), top)
        top = jnp.broadcast_to(jnp.max(top, axis=1, keepdims=True), (tokens, HEAD_WIDTH))
        ones = jnp.ones((tokens, HEAD_WIDTH), jnp.bfloat16)

        def mix(offset, total):
            weight = []
            for c in range(pieces):
                part = scores[offset, :, c * HEAD_WIDTH : (c + 1) * HEAD_WIDTH]
                weight.append(jnp.exp2((part - top) * factor).astype(jnp.bfloat16))
            weight = jnp.concatenate(weight, axis=1)
            value = jnp.concatenate([kvb[offset, 1], ones], axis=1)
            return total + jnp.dot(weight, value, preferred_element_type=jnp.float32)

        total = lax.fori_loop(
            0, nz + 1, mix, jnp.zeros((tokens, 2 * HEAD_WIDTH), jnp.float32)
        )
        out_ref[:, where_h] = (total[:, :HEAD_WIDTH] / total[:, HEAD_WIDTH:]).astype(
            jnp.bfloat16
        )
        return carry

    lax.fori_loop(0, heads, attend, 0)

    def finish(i, carry):
        a_finish(i)
        w_finish(i)
        return carry

    lax.fori_loop(0, nz, finish, 0)
    for step in range(1, nh):
        head_copy(step).wait_send()

    def kv_finish(j, carry):
        reach_up = reach(j)
        for half in range(2):

            @pl.when(j + 1 <= reach_up)
            def _():
                kv_forward(j, half).wait_send()

            @pl.when((j > 0) & (j > reach_up) & (j - 1 > reach_up))
            def _():
                kv_backward(j, half).wait_send()

        return carry

    lax.fori_loop(0, nz + 1, kv_finish, 0)
    for half in range(2):
        kv_cross(half).wait_send()


def body(
    nz,
    nh,
    hidden,
    attention_norm_gain,
    wq,
    adapter_down_weight,
    adapter_up_weight,
    key_value_cache,
    logical_page_table,
    lengths,
    prompt_adapter_index,
):
    tokens, width = hidden.shape
    feat, cols = wq.shape
    own_width = adapter_down_weight.shape[0]
    pages = logical_page_table.shape[1]
    kv = key_value_cache.reshape(pages, tokens // pages, 2 * HEAD_WIDTH)
    half = HEAD_WIDTH // 2
    freq = ROPE_BASE ** (-(jnp.arange(half, dtype=jnp.float32) * 2.0 / HEAD_WIDTH))
    freq = jnp.concatenate([freq, freq])[None, :]
    smem = pl.BlockSpec(memory_space=pltpu.SMEM)
    vmem = pl.BlockSpec(memory_space=pltpu.VMEM)
    dma = pltpu.SemaphoreType.DMA
    bf16, f32, i32 = jnp.bfloat16, jnp.float32, jnp.int32
    return pl.pallas_call(
        functools.partial(kernel, nz, nh),
        name="project_attend",
        out_shape=(
            jax.ShapeDtypeStruct((tokens, cols), bf16),
            jax.ShapeDtypeStruct((tokens, cols), bf16),
        ),
        in_specs=[smem] * 3 + [vmem] * 7,
        out_specs=(vmem, vmem),
        scratch_shapes=[
            pltpu.VMEM((nz, tokens, NX * feat), bf16),
            pltpu.VMEM((tokens, own_width), bf16),
            pltpu.VMEM((nz, NX, 2 * RANK, cols), bf16),
            pltpu.VMEM((nz, NX, feat, cols), bf16),
            pltpu.VMEM((nz + 1, 2, tokens, HEAD_WIDTH), bf16),
            pltpu.VMEM((tokens, cols), f32),
            pltpu.VMEM((tokens, HEAD_WIDTH), i32),
            pltpu.VMEM((tokens, HEAD_WIDTH), i32),
            pltpu.VMEM((8, tokens), i32),
            pltpu.VMEM((tokens, HEAD_WIDTH), f32),
            pltpu.VMEM((tokens, HEAD_WIDTH), f32),
            pltpu.VMEM((RANK, tokens), f32),
            pltpu.VMEM((nh, RANK, tokens), f32),
            pltpu.VMEM((nz + 1, tokens, tokens), f32),
            dma((nz, NX)),
            dma((nz, NX)),
            dma((nz + 1,)),
            dma((nz + 1,)),
            dma((3, nz)),
            dma((3, nz)),
            dma((nz + 1, 2)),
            dma((nz + 1, 2)),
            dma((nz + 1, 2)),
            dma((nh,)),
            dma((nh,)),
        ],
        compiler_params=pltpu.CompilerParams(
            collective_id=0, has_side_effects=True, vmem_limit_bytes=58 << 20
        ),
    )(
        lengths,
        prompt_adapter_index,
        logical_page_table,
        hidden,
        attention_norm_gain[None, :],
        wq,
        adapter_down_weight,
        adapter_up_weight,
        kv,
        freq,
    )


def solution(mesh):
    return jax.shard_map(
        functools.partial(body, mesh.shape["page"] // NX, mesh.shape["head"]),
        mesh=mesh,
        in_specs=(
            P("page", None),
            P(),
            P("page", "head"),
            P("head", "page"),
            P("page", "head"),
            P("page", None, "head"),
            P("page", None),
            P(),
            P(),
        ),
        out_specs=(P("page", "head"), P("page", "head")),
        check_vma=False,
    )
```

```python
import functools
import math

import jax
import jax.numpy as jnp
import numpy as np
from jax import lax
from jax.experimental import pallas as pl
from jax.experimental.pallas import tpu as pltpu
from jax.sharding import PartitionSpec as P

HEAD_WIDTH = 128
RANK = 16
EPSILON = 1e-05
ROPE_BASE = 500000.0
NX = 4
MASKED = -1e30
LAG_NEAR = 2
LAG_FAR = 4
UNROLL = 4


def clamp(value, low, high):
    return jnp.minimum(jnp.maximum(value, low), high)


def kernel(
    nz,
    nh,
    length_ref,
    prompt_adapter_ref,
    table_ref,
    hidden_any,
    gain_ref,
    wq_ref,
    down_ref,
    up_ref,
    kv_ref,
    freq_ref,
    query_ref,
    out_ref,
    hidden_ref,
    gain,
    normed,
    own_feat,
    ga,
    share,
    share_in,
    slots,
    gw,
    kvb,
    acc,
    start_col,
    slot_col,
    slot_row,
    cosine,
    sine,
    psum,
    scores,
    tops,
    hidden_sem,
    recv_a,
    send_a,
    recv_w,
    send_zw,
    send_xw,
    recv_rs,
    send_rs,
    recv_ag,
    send_ag,
    recv_kv,
    send_kf,
    send_kb,
    recv_h,
    send_h,
):
    page_axis = NX * nz
    tokens, width = hidden_ref.shape
    feat = wq_ref.shape[0]
    cols = wq_ref.shape[1]
    heads = cols // HEAD_WIDTH
    own_width = own_feat.shape[1]
    requests = length_ref.shape[0]
    quarter = requests // NX
    pages = kv_ref.shape[0]
    page_rows = kv_ref.shape[1]
    me = lax.axis_index("page")
    head = lax.axis_index("head")
    x = me // nz
    z = me % nz
    z_up = x * nz + (z + 1) % nz
    z_down = x * nz + (z + nz - 1) % nz
    p_up = (me + 1) % page_axis
    p_down = (me + page_axis - 1) % page_axis
    left_x = (x + NX - 1) % NX
    right_x = (x + 1) % NX
    far_x = (x + 2) % NX
    x_up = right_x * nz + z
    x_down = left_x * nz + z
    x_far = far_x * nz + z

    hidden_copy = pltpu.make_async_copy(hidden_any, hidden_ref, hidden_sem)
    hidden_copy.start()

    def send(src, dst, send_sem, recv_sem, page):
        return pltpu.make_async_remote_copy(
            src_ref=src,
            dst_ref=dst,
            send_sem=send_sem,
            recv_sem=recv_sem,
            device_id={"page": page},
            device_id_type=pl.DeviceIdType.MESH,
        )

    barrier = pltpu.get_barrier_semaphore()
    greeted = (z_up, z_down, x_up, x_down, x_far, p_up, p_down)
    for page in greeted:
        pl.semaphore_signal(
            barrier, inc=1, device_id={"page": page}, device_id_type=pl.DeviceIdType.MESH
        )
    for step in range(1, nh):
        pl.semaphore_signal(
            barrier,
            inc=1,
            device_id={"head": (head + step) % nh},
            device_id_type=pl.DeviceIdType.MESH,
        )

    ga[z, 0:RANK, :] = up_ref[...]
    ga[z, RANK : 2 * RANK, :] = down_ref[...]
    gw[z, x] = wq_ref[...]
    for j in range(pages):
        page_block = kv_ref[table_ref[0, j]]
        kvb[0, 0, j * page_rows : (j + 1) * page_rows, :] = page_block[:, :HEAD_WIDTH]
        kvb[0, 1, j * page_rows : (j + 1) * page_rows, :] = page_block[:, HEAD_WIDTH:]
    pl.semaphore_wait(barrier, len(greeted) + nh - 1)

    low = nz * 5 // 16
    high = nz - 1 - low

    def reach(offset):
        return clamp(nz - 1 - (z + 2 * nz - offset) % nz, low, high)

    def kv_forward(offset, half):
        return send(
            kvb.at[offset, half],
            kvb.at[offset + 1, half],
            send_kf.at[offset, half],
            recv_kv.at[offset + 1, half],
            p_up,
        )

    def kv_backward(offset, half):
        return send(
            kvb.at[offset, half],
            kvb.at[offset - 1, half],
            send_kb.at[offset, half],
            recv_kv.at[offset - 1, half],
            p_down,
        )

    def kv_cross(half):
        return send(
            kvb.at[0, half],
            kvb.at[nz, half],
            send_kb.at[0, half],
            recv_kv.at[nz, half],
            x_up,
        )

    def kv_wait(offset, half):
        send(
            kvb.at[0, half],
            kvb.at[offset, half],
            send_kb.at[0, half],
            recv_kv.at[offset, half],
            x_up,
        ).wait_recv()

    def kv_step(j):
        reach_up = reach(j)
        back = nz + 1 - j
        reach_back = reach(back)
        for half in range(2):

            @pl.when(j <= reach_up)
            def _():
                kv_wait(j, half)

                @pl.when(j + 1 <= reach_up)
                def _():
                    kv_forward(j, half).start()

            @pl.when(back > reach_back)
            def _():
                kv_wait(back, half)

                @pl.when(back - 1 > reach_back)
                def _():
                    kv_backward(back, half).start()

    def position(i):
        distance = (i + 1) // 2
        return jnp.where(i % 2 == 1, (z + nz - distance) % nz, (z + distance) % nz)

    def goes_up(i):
        return ((i % 2 == 1) & ((i + 1) // 2 < nz // 2)) | (i == 0)

    def goes_down(i):
        return (i % 2 == 0) & ((i + 1) // 2 < nz // 2 - 1)

    def down_slot(i):
        return jnp.where(i == 0, nz, i)

    def a_copy(i, page, slot):
        zz = position(i)
        return send(ga.at[zz], ga.at[zz], send_a.at[slot], recv_a.at[zz], page)

    def w_copy(i, page, slot):
        zz = position(i)
        return send(gw.at[zz, x], gw.at[zz, x], send_zw.at[slot], recv_w.at[zz, x], page)

    def forward_z(i):
        @pl.when(goes_up(i))
        def _():
            a_copy(i, z_up, i).start()
            w_copy(i, z_up, i).start()

        @pl.when(goes_down(i))
        def _():
            a_copy(i, z_down, down_slot(i)).start()
            w_copy(i, z_down, down_slot(i)).start()

    def arrive_z(i):
        for copy in (a_copy, w_copy):
            copy(i, z_up, i).wait_recv()

            @pl.when(goes_up(i))
            def _():
                copy(i, z_up, i).start()

            @pl.when(goes_down(i))
            def _():
                copy(i, z_down, down_slot(i)).start()

    def x_copy(i, xx, page, which):
        zz = position(i)
        return send(
            gw.at[zz, xx], gw.at[zz, xx], send_xw.at[which, zz], recv_w.at[zz, xx], page
        )

    def spread_x(i):
        x_copy(i, x, x_up, 0).start()
        x_copy(i, x, x_down, 1).start()

    def near(i):
        x_copy(i, left_x, x_up, 2).wait_recv()

        @pl.when(i % 2 == 0)
        def _():
            x_copy(i, left_x, x_up, 2).start()

        x_copy(i, right_x, x_down, 2).wait_recv()

        @pl.when(i % 2 == 1)
        def _():
            x_copy(i, right_x, x_down, 2).start()

    peers = ((right_x, x_up), (left_x, x_down), (far_x, x_far))

    def share_copy(k):
        xx, page = peers[k]
        return send(
            share.at[pl.ds(xx * quarter, quarter)],
            share_in.at[k],
            send_rs.at[k],
            recv_rs.at[k],
            page,
        )

    def slot_copy(k):
        mine = pl.ds(x * quarter, quarter)
        return send(slots.at[mine], slots.at[mine], send_ag.at[k], recv_ag.at[x], peers[k][1])

    def make_share():
        for r in range(requests):
            wanted = prompt_adapter_ref[r] - x * nz
            block = ga[jnp.minimum(jnp.maximum(wanted, 0), nz - 1)].astype(jnp.float32)
            held = jnp.where((wanted >= 0) & (wanted < nz), 1.0, 0.0)
            share[r] = (block * held).astype(jnp.bfloat16)
        for k in range(3):
            share_copy(k).start()

    def sum_share():
        for k in range(3):
            share_copy(k).wait_recv()
        mine = pl.ds(x * quarter, quarter)
        total = share[mine].astype(jnp.float32)
        for k in range(3):
            total = total + share_in[k].astype(jnp.float32)
        slots[mine] = total.astype(jnp.bfloat16)
        for k in range(3):
            slot_copy(k).start()

    def head_copy(step):
        return pltpu.make_async_remote_copy(
            src_ref=psum.at[0],
            dst_ref=psum.at[step],
            send_sem=send_h.at[step],
            recv_sem=recv_h.at[step],
            device_id={"head": (head + step) % nh},
            device_id_type=pl.DeviceIdType.MESH,
        )

    def use_slots():
        for xx in (left_x, right_x, far_x):
            theirs = pl.ds(xx * quarter, quarter)
            send(
                slots.at[theirs], slots.at[theirs], send_ag.at[0], recv_ag.at[xx], x_up
            ).wait_recv()
        part = lax.dot_general(
            slots[:, RANK : 2 * RANK, :].reshape(requests * RANK, cols),
            own_feat[...],
            (((1,), (1,)), ((), ())),
            preferred_element_type=jnp.float32,
        )
        wanted = slot_row[...]
        wanted = jnp.concatenate([wanted, wanted], axis=0)
        total = jnp.zeros((RANK, tokens), jnp.float32)
        for r in range(requests):
            total += jnp.where(wanted == r, part[r * RANK : (r + 1) * RANK], 0.0)
        psum[0] = total
        for step in range(1, nh):
            head_copy(step).start()

    forward_z(0)
    spread_x(0)
    for half in range(2):

        @pl.when(reach(0) >= 1)
        def _():
            kv_forward(0, half).start()

        kv_cross(half).start()

    def prompts(token):
        start = jnp.zeros(token.shape, jnp.int32)
        slot = jnp.zeros(token.shape, jnp.int32)
        end = jnp.int32(0)
        for r in range(requests):
            begin = end
            end = end + length_ref[r]
            inside = token >= begin
            start = jnp.where(inside, begin, start)
            slot = jnp.where(inside, r, slot)
        return start, slot

    slot_row[...] = prompts(
        me * tokens + lax.broadcasted_iota(jnp.int32, (8, tokens), 1)
    )[1]
    gain[...] = gain_ref[...].astype(jnp.float32)
    acc[...] = jnp.zeros_like(acc)
    hidden_copy.wait()

    rows_step = 32
    norm_steps = tokens // rows_step
    norm_each = (norm_steps + LAG_FAR - 1) // LAG_FAR

    def norm_rows(step, carry):
        rows = pl.ds(pl.multiple_of(step * rows_step, rows_step), rows_step)
        value = hidden_ref[rows, :].astype(jnp.float32)
        scale = lax.rsqrt(jnp.mean(value * value, axis=-1, keepdims=True) + EPSILON)
        lane = lax.broadcasted_iota(jnp.int32, (rows_step, 2 * feat), 1)
        lower = lane < feat
        for pair in range(nz // 2):
            piece = []
            for k in range(NX):
                c = k * nz // 2 + pair
                part = value[:, c * 2 * feat : (c + 1) * 2 * feat] * scale
                piece.append(part * gain[c : c + 1, :])
            for k in range(0, NX, 2):
                even = jnp.where(lower, piece[k], pltpu.roll(piece[k + 1], feat, 1))
                odd = jnp.where(lower, pltpu.roll(piece[k], feat, 1), piece[k + 1])
                normed[2 * pair, rows, k * feat : (k + 2) * feat] = even.astype(jnp.bfloat16)
                normed[2 * pair + 1, rows, k * feat : (k + 2) * feat] = odd.astype(jnp.bfloat16)
        for k in range(own_width // HEAD_WIDTH):
            c = head * (own_width // HEAD_WIDTH) + k
            lanes = pl.ds(pl.multiple_of(c * HEAD_WIDTH, HEAD_WIDTH), HEAD_WIDTH)
            own = hidden_ref[rows, lanes].astype(jnp.float32) * scale * gain[pl.ds(c, 1), :]
            own_feat[rows, k * HEAD_WIDTH : (k + 1) * HEAD_WIDTH] = own.astype(jnp.bfloat16)
        token = me * tokens + step * rows_step + lax.broadcasted_iota(
            jnp.int32, (rows_step, HEAD_WIDTH), 0
        )
        start, slot = prompts(token)
        start_col[rows, :] = start
        slot_col[rows, :] = slot
        return carry

    lane = lax.broadcasted_iota(jnp.int32, (tokens, HEAD_WIDTH), 1)

    def rotation():
        token = me * tokens + lax.broadcasted_iota(jnp.int32, (tokens, HEAD_WIDTH), 0)
        angle = (token - start_col[...]).astype(jnp.float32) * freq_ref[...]
        cosine[...] = jnp.cos(angle)
        turn = jnp.sin(angle)
        sine[...] = jnp.where(lane < HEAD_WIDTH // 2, -turn, turn)

    def at(m, when, body):
        @pl.when(m == when)
        def _():
            body()

    last_z = 3 * (nz // 4) - 1 if nz % 4 == 0 else nz // 2
    kv_early = nz // 5

    def weights_step(m, carry):
        distance = 2 * (m // 3) + m % 3

        @pl.when((m % 3 != 0) & (distance <= nz // 2))
        def _():
            arrive_z(2 * distance - 1)

            @pl.when(distance < nz // 2)
            def _():
                arrive_z(2 * distance)

        @pl.when((m >= 1) & (m < nz))
        def _():
            spread_x(m)

        @pl.when((m >= LAG_NEAR) & (m < nz + LAG_NEAR))
        def _():
            near(m - LAG_NEAR)

        @pl.when(m < LAG_FAR)
        def _():
            lax.fori_loop(
                m * norm_each,
                jnp.minimum((m + 1) * norm_each, norm_steps),
                norm_rows,
                0,
            )

        at(m, LAG_FAR + 1, rotation)
        at(m, last_z, make_share)
        at(m, last_z + 2, sum_share)
        at(m, last_z + 4, use_slots)

        @pl.when((m % 3 == 0) & (m >= 3) & (m // 3 <= kv_early))
        def _():
            kv_step(m // 3)

        late = m - 3 * kv_early
        @pl.when((late > 0) & (late % 2 == 1) & (kv_early + (late + 1) // 2 <= nz))
        def _():
            kv_step(kv_early + (late + 1) // 2)

        @pl.when(m >= LAG_FAR)
        def _():
            i = m - LAG_FAR
            zz = position(i)
            x_copy(i, far_x, x_up, 2).wait_recv()
            acc[...] += jnp.dot(
                normed[zz], gw[zz].reshape(NX * feat, cols), preferred_element_type=jnp.float32
            )

        return carry

    count = max(nz + LAG_FAR, last_z + 5)
    assert count == nz + LAG_FAR or nz < 16
    lax.fori_loop(0, nz + LAG_FAR, weights_step, 0)
    if last_z + 4 >= nz + LAG_FAR:
        use_slots()
    kv_next = kv_early + (nz + LAG_FAR - 1 - 3 * kv_early + 1) // 2 + 1

    def service(limit):
        nonlocal kv_next
        while kv_next <= min(limit, nz):
            kv_step(jnp.int32(kv_next))
            kv_next += 1

    first_late = kv_next
    service(first_late)

    for step in range(1, nh):
        head_copy(step).wait_recv()
    shrunk = psum[0]
    for step in range(1, nh):
        shrunk = shrunk + psum[step]
    shrunk = shrunk.astype(jnp.bfloat16).astype(jnp.float32)
    shrunk = jnp.concatenate([shrunk] * (HEAD_WIDTH // RANK), axis=0)
    shrunk = jnp.transpose(shrunk)
    per = HEAD_WIDTH // RANK
    spread = []
    for c in range(requests // per):
        wanted = c * per + lane // RANK
        spread.append(jnp.where(slot_col[...] == wanted, shrunk, 0.0).astype(jnp.bfloat16))
    spread = jnp.concatenate(spread, axis=1)
    acc[...] += jnp.dot(
        spread,
        slots[:, 0:RANK, :].reshape(requests * RANK, cols),
        preferred_element_type=jnp.float32,
    )

    for h in range(heads):
        u = acc[:, h * HEAD_WIDTH : (h + 1) * HEAD_WIDTH]
        turned = u * cosine[...] + pltpu.roll(u, HEAD_WIDTH // 2, 1) * sine[...]
        query_ref[:, h * HEAD_WIDTH : (h + 1) * HEAD_WIDTH] = turned.astype(jnp.bfloat16)

    service(first_late + 1)

    factor = math.log2(math.e) / math.sqrt(HEAD_WIDTH)
    begin = start_col[...] - lane
    row = lax.broadcasted_iota(jnp.int32, (tokens, HEAD_WIDTH), 0)
    pieces = tokens // HEAD_WIDTH
    ones = jnp.ones((tokens, HEAD_WIDTH), jnp.bfloat16)

    def lanes_of(h):
        return pl.ds(pl.multiple_of(h * HEAD_WIDTH, HEAD_WIDTH), HEAD_WIDTH)

    def score(h, buffer, offset, top, causal):
        block = lax.dot_general(
            query_ref[:, lanes_of(h)],
            kvb[offset, 0],
            (((1,), (1,)), ((), ())),
            preferred_element_type=jnp.float32,
        )
        base = (me - offset) * tokens
        for c in range(pieces):
            visible = begin <= base + c * HEAD_WIDTH
            if causal:
                visible = visible & (lane + c * HEAD_WIDTH <= row)
            part = block[:, c * HEAD_WIDTH : (c + 1) * HEAD_WIDTH]
            part = jnp.where(visible, part, MASKED)
            scores[buffer, offset, :, c * HEAD_WIDTH : (c + 1) * HEAD_WIDTH] = part
            top = part if top is None else jnp.maximum(top, part)
        return top

    def score_early(h, buffer):
        top = score(h, buffer, 0, None, True)

        def one(k, top):
            offset = jnp.where(k < low, k + 1, nz - 2 * low + 1 + k)
            return score(h, buffer, offset, top, False)

        tops[buffer] = lax.fori_loop(0, 2 * low, one, top, unroll=UNROLL)

    def score_late(h, buffer):
        return lax.fori_loop(
            low + 1,
            nz - low + 1,
            lambda o, t: score(h, buffer, o, t, False),
            tops[buffer],
            unroll=UNROLL,
        )

    def finish_head(h, buffer, top):
        top = jnp.broadcast_to(jnp.max(top, axis=1, keepdims=True), (tokens, HEAD_WIDTH))

        def mix(offset, total):
            weight = []
            for c in range(pieces):
                part = scores[buffer, offset, :, c * HEAD_WIDTH : (c + 1) * HEAD_WIDTH]
                weight.append(jnp.exp2((part - top) * factor).astype(jnp.bfloat16))
            weight = jnp.concatenate(weight, axis=1)
            value = jnp.concatenate([kvb[offset, 1], ones], axis=1)
            return total + jnp.dot(weight, value, preferred_element_type=jnp.float32)

        total = lax.fori_loop(
            0,
            nz + 1,
            mix,
            jnp.zeros((tokens, 2 * HEAD_WIDTH), jnp.float32),
            unroll=UNROLL,
        )
        out_ref[:, lanes_of(h)] = (total[:, :HEAD_WIDTH] / total[:, HEAD_WIDTH:]).astype(
            jnp.bfloat16
        )

    score_early(0, 0)
    service(first_late + 2)
    score_early(1, 1)
    service(nz)

    def attend(h, carry):
        buffer = h % 2

        @pl.when(h >= 2)
        def _():
            score_early(h, buffer)

        finish_head(h, buffer, score_late(h, buffer))
        return carry

    lax.fori_loop(0, heads, attend, 0)

    def finish(i, carry):
        @pl.when(goes_up(i))
        def _():
            a_copy(i, z_up, i).wait_send()
            w_copy(i, z_up, i).wait_send()

        @pl.when(goes_down(i))
        def _():
            a_copy(i, z_down, down_slot(i)).wait_send()
            w_copy(i, z_down, down_slot(i)).wait_send()

        x_copy(i, x, x_up, 0).wait_send()
        x_copy(i, x, x_down, 1).wait_send()
        x_copy(i, left_x, x_up, 2).wait_send()
        return carry

    lax.fori_loop(0, nz, finish, 0)
    for k in range(3):
        share_copy(k).wait_send()
        slot_copy(k).wait_send()
    for step in range(1, nh):
        head_copy(step).wait_send()

    def kv_finish(j, carry):
        reach_up = reach(j)
        for half in range(2):

            @pl.when(j + 1 <= reach_up)
            def _():
                kv_forward(j, half).wait_send()

            @pl.when(j - 1 > reach_up)
            def _():
                kv_backward(j, half).wait_send()

        return carry

    lax.fori_loop(0, nz + 1, kv_finish, 0)
    for half in range(2):
        kv_cross(half).wait_send()


def body(
    nz,
    nh,
    hidden,
    attention_norm_gain,
    wq,
    adapter_down_weight,
    adapter_up_weight,
    key_value_cache,
    logical_page_table,
    lengths,
    prompt_adapter_index,
):
    tokens, width = hidden.shape
    feat, cols = wq.shape
    own_width = adapter_down_weight.shape[0]
    pages = logical_page_table.shape[1]
    requests = lengths.shape[0]
    kv = key_value_cache.reshape(pages, tokens // pages, 2 * HEAD_WIDTH)
    half = HEAD_WIDTH // 2
    freq = ROPE_BASE ** (-(np.arange(half, dtype=np.float64) * 2.0 / HEAD_WIDTH))
    freq = np.concatenate([freq, freq])[None, :].astype(np.float32)
    smem = pl.BlockSpec(memory_space=pltpu.SMEM)
    vmem = pl.BlockSpec(memory_space=pltpu.VMEM)
    dma = pltpu.SemaphoreType.DMA
    bf16, f32, i32 = jnp.bfloat16, jnp.float32, jnp.int32
    return pl.pallas_call(
        functools.partial(kernel, nz, nh),
        name="project_attend",
        out_shape=(
            jax.ShapeDtypeStruct((tokens, cols), bf16),
            jax.ShapeDtypeStruct((tokens, cols), bf16),
        ),
        in_specs=[smem] * 3 + [pl.BlockSpec(memory_space=pl.ANY)] + [vmem] * 6,
        out_specs=(vmem, vmem),
        scratch_shapes=[
            pltpu.VMEM((tokens, width), bf16),
            pltpu.VMEM((width // HEAD_WIDTH, HEAD_WIDTH), f32),
            pltpu.VMEM((nz, tokens, NX * feat), bf16),
            pltpu.VMEM((tokens, own_width), bf16),
            pltpu.VMEM((nz, 2 * RANK, cols), bf16),
            pltpu.VMEM((requests, 2 * RANK, cols), bf16),
            pltpu.VMEM((3, requests // NX, 2 * RANK, cols), bf16),
            pltpu.VMEM((requests, 2 * RANK, cols), bf16),
            pltpu.VMEM((nz, NX, feat, cols), bf16),
            pltpu.VMEM((nz + 1, 2, tokens, HEAD_WIDTH), bf16),
            pltpu.VMEM((tokens, cols), f32),
            pltpu.VMEM((tokens, HEAD_WIDTH), i32),
            pltpu.VMEM((tokens, HEAD_WIDTH), i32),
            pltpu.VMEM((8, tokens), i32),
            pltpu.VMEM((tokens, HEAD_WIDTH), f32),
            pltpu.VMEM((tokens, HEAD_WIDTH), f32),
            pltpu.VMEM((nh, RANK, tokens), f32),
            pltpu.VMEM((2, nz + 1, tokens, tokens), f32),
            pltpu.VMEM((2, tokens, HEAD_WIDTH), f32),
            dma(()),
            dma((nz,)),
            dma((nz + 1,)),
            dma((nz, NX)),
            dma((nz + 1,)),
            dma((3, nz)),
            dma((3,)),
            dma((3,)),
            dma((NX,)),
            dma((3,)),
            dma((nz + 1, 2)),
            dma((nz + 1, 2)),
            dma((nz + 1, 2)),
            dma((nh,)),
            dma((nh,)),
        ],
        compiler_params=pltpu.CompilerParams(
            collective_id=0, has_side_effects=True, vmem_limit_bytes=58 << 20
        ),
    )(
        lengths,
        prompt_adapter_index,
        logical_page_table,
        hidden,
        attention_norm_gain.reshape(width // HEAD_WIDTH, HEAD_WIDTH),
        wq,
        adapter_down_weight.T,
        adapter_up_weight,
        kv,
        freq,
    )


def solution(mesh):
    return jax.shard_map(
        functools.partial(body, mesh.shape["page"] // NX, mesh.shape["head"]),
        mesh=mesh,
        in_specs=(
            P("page", None),
            P(),
            P("page", "head"),
            P("head", "page"),
            P("page", "head"),
            P("page", None, "head"),
            P("page", None),
            P(),
            P(),
        ),
        out_specs=(P("page", "head"), P("page", "head")),
        check_vma=False,
    )
```

```python
import functools
import math

import jax
import jax.numpy as jnp
import numpy as np
from jax import lax
from jax.experimental import pallas as pl
from jax.experimental.pallas import tpu as pltpu
from jax.sharding import PartitionSpec as P

HEAD_WIDTH = 128
RANK = 16
EPSILON = 1e-05
ROPE_BASE = 500000.0
NX = 4
MASKED = -1e30
LAG_NEAR = 2
LAG_FAR = 4
GROUP = 2
UNROLL = 3
STACK = 2


def clamp(value, low, high):
    return jnp.minimum(jnp.maximum(value, low), high)


def kernel(
    nz,
    nh,
    length_ref,
    prompt_adapter_ref,
    table_ref,
    hidden_any,
    gain_ref,
    wq_ref,
    down_ref,
    up_ref,
    kv_ref,
    freq_ref,
    query_ref,
    out_ref,
    hidden_ref,
    gain,
    normed,
    own_feat,
    ga,
    share,
    share_in,
    slots,
    gw,
    kvb,
    acc,
    start_col,
    slot_col,
    slot_row,
    cosine,
    sine,
    psum,
    scores,
    tops,
    totals,
    stacked,
    hidden_sem,
    recv_a,
    send_a,
    recv_w,
    send_zw,
    send_xw,
    recv_rs,
    send_rs,
    recv_ag,
    send_ag,
    recv_kv,
    send_kf,
    send_kb,
    recv_h,
    send_h,
):
    page_axis = NX * nz
    tokens, width = hidden_ref.shape
    feat = wq_ref.shape[0]
    cols = wq_ref.shape[1]
    heads = cols // HEAD_WIDTH
    own_width = own_feat.shape[1]
    requests = length_ref.shape[0]
    quarter = requests // NX
    pages = kv_ref.shape[0]
    page_rows = kv_ref.shape[1]
    me = lax.axis_index("page")
    head = lax.axis_index("head")
    x = me // nz
    z = me % nz
    z_up = x * nz + (z + 1) % nz
    z_down = x * nz + (z + nz - 1) % nz
    p_up = (me + 1) % page_axis
    p_down = (me + page_axis - 1) % page_axis
    left_x = (x + NX - 1) % NX
    right_x = (x + 1) % NX
    far_x = (x + 2) % NX
    x_up = right_x * nz + z
    x_down = left_x * nz + z
    x_far = far_x * nz + z

    hidden_copy = pltpu.make_async_copy(hidden_any, hidden_ref, hidden_sem)
    hidden_copy.start()

    def send(src, dst, send_sem, recv_sem, page):
        return pltpu.make_async_remote_copy(
            src_ref=src,
            dst_ref=dst,
            send_sem=send_sem,
            recv_sem=recv_sem,
            device_id={"page": page},
            device_id_type=pl.DeviceIdType.MESH,
        )

    barrier = pltpu.get_barrier_semaphore()
    greeted = (z_up, z_down, x_up, x_down, x_far, p_up, p_down)
    for page in greeted:
        pl.semaphore_signal(
            barrier, inc=1, device_id={"page": page}, device_id_type=pl.DeviceIdType.MESH
        )
    for step in range(1, nh):
        pl.semaphore_signal(
            barrier,
            inc=1,
            device_id={"head": (head + step) % nh},
            device_id_type=pl.DeviceIdType.MESH,
        )

    ga[z, 0:RANK, :] = up_ref[...]
    ga[z, RANK : 2 * RANK, :] = down_ref[...]
    gw[z, x] = wq_ref[...]
    for j in range(pages):
        page_block = kv_ref[table_ref[0, j]]
        kvb[0, 0, j * page_rows : (j + 1) * page_rows, :] = page_block[:, :HEAD_WIDTH]
        kvb[0, 1, j * page_rows : (j + 1) * page_rows, :] = page_block[:, HEAD_WIDTH:]
    pl.semaphore_wait(barrier, len(greeted) + nh - 1)

    low = nz // 4
    high = nz - 1 - low

    def reach(offset):
        return clamp(nz - 1 - (z + 2 * nz - offset) % nz, low, high)

    def kv_forward(offset, half):
        return send(
            kvb.at[offset, half],
            kvb.at[offset + 1, half],
            send_kf.at[offset, half],
            recv_kv.at[offset + 1, half],
            p_up,
        )

    def kv_backward(offset, half):
        return send(
            kvb.at[offset, half],
            kvb.at[offset - 1, half],
            send_kb.at[offset, half],
            recv_kv.at[offset - 1, half],
            p_down,
        )

    def kv_cross(half):
        return send(
            kvb.at[0, half],
            kvb.at[nz, half],
            send_kb.at[0, half],
            recv_kv.at[nz, half],
            x_up,
        )

    def kv_wait(offset, half):
        send(
            kvb.at[0, half],
            kvb.at[offset, half],
            send_kb.at[0, half],
            recv_kv.at[offset, half],
            x_up,
        ).wait_recv()

    def kv_half(j, half):
        reach_up = reach(j)
        back = nz + 1 - j
        reach_back = reach(back)

        @pl.when(j <= reach_up)
        def _():
            kv_wait(j, half)

            @pl.when(j + 1 <= reach_up)
            def _():
                kv_forward(j, half).start()

        @pl.when(back > reach_back)
        def _():
            kv_wait(back, half)

            @pl.when(back - 1 > reach_back)
            def _():
                kv_backward(back, half).start()

    def kv_step(j):
        kv_half(j, 0)
        kv_half(j, 1)

    def position(i):
        distance = (i + 1) // 2
        return jnp.where(i % 2 == 1, (z + nz - distance) % nz, (z + distance) % nz)

    def goes_up(i):
        return ((i % 2 == 1) & ((i + 1) // 2 < nz // 2)) | (i == 0)

    def goes_down(i):
        return (i % 2 == 0) & ((i + 1) // 2 < nz // 2 - 1)

    def down_slot(i):
        return jnp.where(i == 0, nz, i)

    def a_copy(i, page, slot):
        zz = position(i)
        return send(ga.at[zz], ga.at[zz], send_a.at[slot], recv_a.at[zz], page)

    def w_copy(i, page, slot):
        zz = position(i)
        return send(gw.at[zz, x], gw.at[zz, x], send_zw.at[slot], recv_w.at[zz, x], page)

    def forward_z(i):
        @pl.when(goes_up(i))
        def _():
            a_copy(i, z_up, i).start()
            w_copy(i, z_up, i).start()

        @pl.when(goes_down(i))
        def _():
            a_copy(i, z_down, down_slot(i)).start()
            w_copy(i, z_down, down_slot(i)).start()

    def arrive_z(i):
        for copy in (a_copy, w_copy):
            copy(i, z_up, i).wait_recv()

            @pl.when(goes_up(i))
            def _():
                copy(i, z_up, i).start()

            @pl.when(goes_down(i))
            def _():
                copy(i, z_down, down_slot(i)).start()

    def x_copy(i, xx, page, which):
        zz = position(i)
        return send(
            gw.at[zz, xx], gw.at[zz, xx], send_xw.at[which, zz], recv_w.at[zz, xx], page
        )

    def spread_x(i):
        x_copy(i, x, x_up, 0).start()
        x_copy(i, x, x_down, 1).start()

    def near(i):
        x_copy(i, left_x, x_up, 2).wait_recv()

        @pl.when(i % 2 == 0)
        def _():
            x_copy(i, left_x, x_up, 2).start()

        x_copy(i, right_x, x_down, 2).wait_recv()

        @pl.when(i % 2 == 1)
        def _():
            x_copy(i, right_x, x_down, 2).start()

    peers = ((right_x, x_up), (left_x, x_down), (far_x, x_far))

    def share_copy(k):
        xx, page = peers[k]
        return send(
            share.at[pl.ds(xx * quarter, quarter)],
            share_in.at[k],
            send_rs.at[k],
            recv_rs.at[k],
            page,
        )

    def slot_copy(k):
        mine = pl.ds(x * quarter, quarter)
        return send(slots.at[mine], slots.at[mine], send_ag.at[k], recv_ag.at[x], peers[k][1])

    def make_share():
        for r in range(requests):
            wanted = prompt_adapter_ref[r] - x * nz
            block = ga[jnp.minimum(jnp.maximum(wanted, 0), nz - 1)].astype(jnp.float32)
            held = jnp.where((wanted >= 0) & (wanted < nz), 1.0, 0.0)
            share[r] = (block * held).astype(jnp.bfloat16)
        for k in range(3):
            share_copy(k).start()

    def sum_share():
        for k in range(3):
            share_copy(k).wait_recv()
        mine = pl.ds(x * quarter, quarter)
        total = share[mine].astype(jnp.float32)
        for k in range(3):
            total = total + share_in[k].astype(jnp.float32)
        slots[mine] = total.astype(jnp.bfloat16)
        for k in range(3):
            slot_copy(k).start()

    def head_copy(step):
        return pltpu.make_async_remote_copy(
            src_ref=psum.at[0],
            dst_ref=psum.at[step],
            send_sem=send_h.at[step],
            recv_sem=recv_h.at[step],
            device_id={"head": (head + step) % nh},
            device_id_type=pl.DeviceIdType.MESH,
        )

    def use_slots():
        for xx in (left_x, right_x, far_x):
            theirs = pl.ds(xx * quarter, quarter)
            send(
                slots.at[theirs], slots.at[theirs], send_ag.at[0], recv_ag.at[xx], x_up
            ).wait_recv()
        part = lax.dot_general(
            slots[:, RANK : 2 * RANK, :].reshape(requests * RANK, cols),
            own_feat[...],
            (((1,), (1,)), ((), ())),
            preferred_element_type=jnp.float32,
        )
        wanted = slot_row[...]
        wanted = jnp.concatenate([wanted, wanted], axis=0)
        total = jnp.zeros((RANK, tokens), jnp.float32)
        for r in range(requests):
            total += jnp.where(wanted == r, part[r * RANK : (r + 1) * RANK], 0.0)
        psum[0] = total
        for step in range(1, nh):
            head_copy(step).start()

    forward_z(0)
    spread_x(0)
    for half in range(2):

        @pl.when(reach(0) >= 1)
        def _():
            kv_forward(0, half).start()

        kv_cross(half).start()

    def prompts(token):
        start = jnp.zeros(token.shape, jnp.int32)
        slot = jnp.zeros(token.shape, jnp.int32)
        end = jnp.int32(0)
        for r in range(requests):
            begin = end
            end = end + length_ref[r]
            inside = token >= begin
            start = jnp.where(inside, begin, start)
            slot = jnp.where(inside, r, slot)
        return start, slot

    slot_row[...] = prompts(
        me * tokens + lax.broadcasted_iota(jnp.int32, (8, tokens), 1)
    )[1]
    gain[...] = gain_ref[...].astype(jnp.float32)
    acc[...] = jnp.zeros_like(acc)
    hidden_copy.wait()

    rows_step = 32
    norm_steps = tokens // rows_step
    norm_each = (norm_steps + LAG_FAR - 1) // LAG_FAR

    def norm_rows(step, carry):
        rows = pl.ds(pl.multiple_of(step * rows_step, rows_step), rows_step)
        value = hidden_ref[rows, :].astype(jnp.float32)
        scale = lax.rsqrt(jnp.mean(value * value, axis=-1, keepdims=True) + EPSILON)
        lane = lax.broadcasted_iota(jnp.int32, (rows_step, 2 * feat), 1)
        lower = lane < feat
        for pair in range(nz // 2):
            piece = []
            for k in range(NX):
                c = k * nz // 2 + pair
                part = value[:, c * 2 * feat : (c + 1) * 2 * feat] * scale
                piece.append(part * gain[c : c + 1, :])
            for k in range(0, NX, 2):
                even = jnp.where(lower, piece[k], pltpu.roll(piece[k + 1], feat, 1))
                odd = jnp.where(lower, pltpu.roll(piece[k], feat, 1), piece[k + 1])
                normed[2 * pair, rows, k * feat : (k + 2) * feat] = even.astype(jnp.bfloat16)
                normed[2 * pair + 1, rows, k * feat : (k + 2) * feat] = odd.astype(jnp.bfloat16)
        for k in range(own_width // HEAD_WIDTH):
            c = head * (own_width // HEAD_WIDTH) + k
            lanes = pl.ds(pl.multiple_of(c * HEAD_WIDTH, HEAD_WIDTH), HEAD_WIDTH)
            own = hidden_ref[rows, lanes].astype(jnp.float32) * scale * gain[pl.ds(c, 1), :]
            own_feat[rows, k * HEAD_WIDTH : (k + 1) * HEAD_WIDTH] = own.astype(jnp.bfloat16)
        token = me * tokens + step * rows_step + lax.broadcasted_iota(
            jnp.int32, (rows_step, HEAD_WIDTH), 0
        )
        start, slot = prompts(token)
        start_col[rows, :] = start
        slot_col[rows, :] = slot
        return carry

    lane = lax.broadcasted_iota(jnp.int32, (tokens, HEAD_WIDTH), 1)

    def rotation():
        token = me * tokens + lax.broadcasted_iota(jnp.int32, (tokens, HEAD_WIDTH), 0)
        angle = (token - start_col[...]).astype(jnp.float32) * freq_ref[...]
        cosine[...] = jnp.cos(angle)
        turn = jnp.sin(angle)
        sine[...] = jnp.where(lane < HEAD_WIDTH // 2, -turn, turn)

    def at(m, when, body):
        @pl.when(m == when)
        def _():
            body()

    last_z = 3 * (nz // 4) - 1 if nz % 4 == 0 else nz // 2
    kv_early = nz // 5

    def weights_step(m, carry):
        distance = 2 * (m // 3) + m % 3

        @pl.when((m % 3 != 0) & (distance <= nz // 2))
        def _():
            arrive_z(2 * distance - 1)

            @pl.when(distance < nz // 2)
            def _():
                arrive_z(2 * distance)

        @pl.when((m >= 1) & (m < nz))
        def _():
            spread_x(m)

        @pl.when((m >= LAG_NEAR) & (m < nz + LAG_NEAR))
        def _():
            near(m - LAG_NEAR)

        @pl.when(m < LAG_FAR)
        def _():
            lax.fori_loop(
                m * norm_each,
                jnp.minimum((m + 1) * norm_each, norm_steps),
                norm_rows,
                0,
            )

        at(m, LAG_FAR + 1, rotation)
        at(m, last_z, make_share)
        at(m, last_z + 2, sum_share)
        at(m, last_z + 4, use_slots)

        @pl.when((m % 3 == 0) & (m >= 3) & (m // 3 <= kv_early))
        def _():
            kv_step(m // 3)

        late = m - 3 * kv_early - 1

        @pl.when((late >= 0) & (kv_early + late // 2 + 1 <= nz))
        def _():
            kv_half(kv_early + late // 2 + 1, late % 2)

        @pl.when(m >= LAG_FAR)
        def _():
            i = m - LAG_FAR
            zz = position(i)
            x_copy(i, far_x, x_up, 2).wait_recv()
            acc[...] += jnp.dot(
                normed[zz], gw[zz].reshape(NX * feat, cols), preferred_element_type=jnp.float32
            )

        return carry

    lax.fori_loop(0, nz + LAG_FAR, weights_step, 0)
    kv_next = kv_early + (nz + LAG_FAR - 1 - 3 * kv_early) // 2 + 1

    def service(limit):
        nonlocal kv_next
        while kv_next <= min(limit, nz):
            kv_step(jnp.int32(kv_next))
            kv_next += 1

    first_late = kv_next
    service(first_late)

    for step in range(1, nh):
        head_copy(step).wait_recv()
    shrunk = psum[0]
    for step in range(1, nh):
        shrunk = shrunk + psum[step]
    shrunk = shrunk.astype(jnp.bfloat16).astype(jnp.float32)
    shrunk = jnp.concatenate([shrunk] * (HEAD_WIDTH // RANK), axis=0)
    shrunk = jnp.transpose(shrunk)
    per = HEAD_WIDTH // RANK
    spread = []
    for c in range(requests // per):
        wanted = c * per + lane // RANK
        spread.append(jnp.where(slot_col[...] == wanted, shrunk, 0.0).astype(jnp.bfloat16))
    spread = jnp.concatenate(spread, axis=1)
    acc[...] += jnp.dot(
        spread,
        slots[:, 0:RANK, :].reshape(requests * RANK, cols),
        preferred_element_type=jnp.float32,
    )

    for h in range(heads):
        u = acc[:, h * HEAD_WIDTH : (h + 1) * HEAD_WIDTH]
        turned = u * cosine[...] + pltpu.roll(u, HEAD_WIDTH // 2, 1) * sine[...]
        turned = turned.astype(jnp.bfloat16)
        query_ref[:, h * HEAD_WIDTH : (h + 1) * HEAD_WIDTH] = turned
        stacked[h // STACK, (h % STACK) * tokens : (h % STACK + 1) * tokens, :] = turned

    service(first_late + 1)

    factor = math.log2(math.e) / math.sqrt(HEAD_WIDTH)
    begin = start_col[...] - lane
    row = lax.broadcasted_iota(jnp.int32, (tokens, HEAD_WIDTH), 0)
    pieces = tokens // HEAD_WIDTH
    done = min(first_late + 1, nz)

    def at_hand(offset):
        return offset <= low or offset > nz - low or max(offset, nz + 1 - offset) <= done

    def groups(offsets):
        found = []
        for offset in offsets:
            if found and len(found[-1]) < GROUP and found[-1][-1] + 1 == offset:
                found[-1].append(offset)
            else:
                found.append([offset])
        return found

    early = groups([o for o in range(1, nz + 1) if at_hand(o)])
    late = groups([o for o in range(1, nz + 1) if not at_hand(o)])

    def rows_of(k):
        return slice(k * tokens, (k + 1) * tokens)

    def each(parts, body):
        pairs = [part[0] for part in parts if len(part) == GROUP]

        def one(k, carry):
            offset = jnp.int32(pairs[0])
            for other, start in enumerate(pairs):
                offset = jnp.where(k == other, start, offset)
            body(offset, GROUP)
            return carry

        if pairs:
            lax.fori_loop(0, len(pairs), one, 0, unroll=UNROLL)
        for part in parts:
            if len(part) < GROUP:
                body(part[0], len(part))

    def block_of(offset, count, half):
        return kvb[pl.ds(offset, count), half].reshape(count * tokens, HEAD_WIDTH)

    def score(b, offset, count, own=False):
        block = lax.dot_general(
            stacked[b],
            block_of(offset, count, 0),
            (((1,), (1,)), ((), ())),
            preferred_element_type=jnp.float32,
        )
        for g in range(count):
            base = (me - offset - g) * tokens
            seen = []
            for c in range(pieces):
                visible = begin <= base + c * HEAD_WIDTH
                if own:
                    visible = visible & (lane + c * HEAD_WIDTH <= row)
                seen.append(visible)
            for k in range(STACK):
                top = None if own else tops[b, rows_of(k), :]
                for c in range(pieces):
                    first = (g * pieces + c) * HEAD_WIDTH
                    part = block[rows_of(k), first : first + HEAD_WIDTH]
                    part = jnp.where(seen[c], part, MASKED)
                    scores[
                        offset + g, rows_of(k), c * HEAD_WIDTH : (c + 1) * HEAD_WIDTH
                    ] = part
                    top = part if top is None else jnp.maximum(top, part)
                tops[b, rows_of(k), :] = top

    def level(b):
        for k in range(STACK):
            tops[b, rows_of(k), :] = jnp.broadcast_to(
                jnp.max(tops[b, rows_of(k), :], axis=1, keepdims=True), (tokens, HEAD_WIDTH)
            )

    def mix(b, offset, count, own=False):
        weight = []
        for g in range(count):
            for c in range(pieces):
                part = scores[offset + g, :, c * HEAD_WIDTH : (c + 1) * HEAD_WIDTH]
                weight.append(jnp.exp2((part - tops[b]) * factor).astype(jnp.bfloat16))
        weight = jnp.concatenate(weight, axis=1)
        value = block_of(offset, count, 1)
        value = jnp.concatenate([value, jnp.ones_like(value)], axis=1)
        product = jnp.dot(weight, value, preferred_element_type=jnp.float32)
        totals[b] = product if own else totals[b] + product

    def serve(j):
        @pl.when(j <= nz)
        def _():
            kv_step(jnp.minimum(j, nz))

    def attend_early(b, carry):
        score(b, 0, 1, True)
        each(early, lambda o, n: score(b, o, n))
        level(b)
        serve(done + 1 + 2 * b)
        mix(b, 0, 1, True)
        each(early, lambda o, n: mix(b, o, n))
        serve(done + 2 + 2 * b)
        return carry

    def attend_late(b, carry):
        if late:
            before = tops[b]
            each(late, lambda o, n: score(b, o, n))
            level(b)
            fade = jnp.exp2((before - tops[b]) * factor)
            totals[b] = totals[b] * jnp.concatenate([fade, fade], axis=1)
            each(late, lambda o, n: mix(b, o, n))
        for k in range(STACK):
            total = totals[b, rows_of(k), :]
            h = b * STACK + k
            out_ref[:, pl.ds(pl.multiple_of(h * HEAD_WIDTH, HEAD_WIDTH), HEAD_WIDTH)] = (
                total[:, :HEAD_WIDTH] / total[:, HEAD_WIDTH:]
            ).astype(jnp.bfloat16)
        return carry

    stacks = heads // STACK
    lax.fori_loop(0, stacks, attend_early, 0)
    kv_next = done + 1 + 2 * stacks
    service(nz)
    lax.fori_loop(0, stacks, attend_late, 0)

    def finish(i, carry):
        @pl.when(goes_up(i))
        def _():
            a_copy(i, z_up, i).wait_send()
            w_copy(i, z_up, i).wait_send()

        @pl.when(goes_down(i))
        def _():
            a_copy(i, z_down, down_slot(i)).wait_send()
            w_copy(i, z_down, down_slot(i)).wait_send()

        x_copy(i, x, x_up, 0).wait_send()
        x_copy(i, x, x_down, 1).wait_send()
        x_copy(i, left_x, x_up, 2).wait_send()
        return carry

    lax.fori_loop(0, nz, finish, 0)
    for k in range(3):
        share_copy(k).wait_send()
        slot_copy(k).wait_send()
    for step in range(1, nh):
        head_copy(step).wait_send()

    def kv_finish(j, carry):
        reach_up = reach(j)
        for half in range(2):

            @pl.when(j + 1 <= reach_up)
            def _():
                kv_forward(j, half).wait_send()

            @pl.when(j - 1 > reach_up)
            def _():
                kv_backward(j, half).wait_send()

        return carry

    lax.fori_loop(0, nz + 1, kv_finish, 0)
    for half in range(2):
        kv_cross(half).wait_send()


def body(
    nz,
    nh,
    hidden,
    attention_norm_gain,
    wq,
    adapter_down_weight,
    adapter_up_weight,
    key_value_cache,
    logical_page_table,
    lengths,
    prompt_adapter_index,
):
    tokens, width = hidden.shape
    feat, cols = wq.shape
    own_width = adapter_down_weight.shape[0]
    pages = logical_page_table.shape[1]
    requests = lengths.shape[0]
    stacks = cols // HEAD_WIDTH // STACK
    kv = key_value_cache.reshape(pages, tokens // pages, 2 * HEAD_WIDTH)
    half = HEAD_WIDTH // 2
    freq = ROPE_BASE ** (-(np.arange(half, dtype=np.float64) * 2.0 / HEAD_WIDTH))
    freq = np.concatenate([freq, freq])[None, :].astype(np.float32)
    smem = pl.BlockSpec(memory_space=pltpu.SMEM)
    vmem = pl.BlockSpec(memory_space=pltpu.VMEM)
    dma = pltpu.SemaphoreType.DMA
    bf16, f32, i32 = jnp.bfloat16, jnp.float32, jnp.int32
    return pl.pallas_call(
        functools.partial(kernel, nz, nh),
        name="project_attend",
        out_shape=(
            jax.ShapeDtypeStruct((tokens, cols), bf16),
            jax.ShapeDtypeStruct((tokens, cols), bf16),
        ),
        in_specs=[smem] * 3 + [pl.BlockSpec(memory_space=pl.ANY)] + [vmem] * 6,
        out_specs=(vmem, vmem),
        scratch_shapes=[
            pltpu.VMEM((tokens, width), bf16),
            pltpu.VMEM((width // HEAD_WIDTH, HEAD_WIDTH), f32),
            pltpu.VMEM((nz, tokens, NX * feat), bf16),
            pltpu.VMEM((tokens, own_width), bf16),
            pltpu.VMEM((nz, 2 * RANK, cols), bf16),
            pltpu.VMEM((requests, 2 * RANK, cols), bf16),
            pltpu.VMEM((3, requests // NX, 2 * RANK, cols), bf16),
            pltpu.VMEM((requests, 2 * RANK, cols), bf16),
            pltpu.VMEM((nz, NX, feat, cols), bf16),
            pltpu.VMEM((nz + 1, 2, tokens, HEAD_WIDTH), bf16),
            pltpu.VMEM((tokens, cols), f32),
            pltpu.VMEM((tokens, HEAD_WIDTH), i32),
            pltpu.VMEM((tokens, HEAD_WIDTH), i32),
            pltpu.VMEM((8, tokens), i32),
            pltpu.VMEM((tokens, HEAD_WIDTH), f32),
            pltpu.VMEM((tokens, HEAD_WIDTH), f32),
            pltpu.VMEM((nh, RANK, tokens), f32),
            pltpu.VMEM((nz + 1, STACK * tokens, tokens), f32),
            pltpu.VMEM((stacks, STACK * tokens, HEAD_WIDTH), f32),
            pltpu.VMEM((stacks, STACK * tokens, 2 * HEAD_WIDTH), f32),
            pltpu.VMEM((stacks, STACK * tokens, HEAD_WIDTH), bf16),
            dma(()),
            dma((nz,)),
            dma((nz + 1,)),
            dma((nz, NX)),
            dma((nz + 1,)),
            dma((3, nz)),
            dma((3,)),
            dma((3,)),
            dma((NX,)),
            dma((3,)),
            dma((nz + 1, 2)),
            dma((nz + 1, 2)),
            dma((nz + 1, 2)),
            dma((nh,)),
            dma((nh,)),
        ],
        compiler_params=pltpu.CompilerParams(
            collective_id=0, has_side_effects=True, vmem_limit_bytes=58 << 20
        ),
    )(
        lengths,
        prompt_adapter_index,
        logical_page_table,
        hidden,
        attention_norm_gain.reshape(width // HEAD_WIDTH, HEAD_WIDTH),
        wq,
        adapter_down_weight.T,
        adapter_up_weight,
        kv,
        freq,
    )


def solution(mesh):
    return jax.shard_map(
        functools.partial(body, mesh.shape["page"] // NX, mesh.shape["head"]),
        mesh=mesh,
        in_specs=(
            P("page", None),
            P(),
            P("page", "head"),
            P("head", "page"),
            P("page", "head"),
            P("page", None, "head"),
            P("page", None),
            P(),
            P(),
        ),
        out_specs=(P("page", "head"), P("page", "head")),
        check_vma=False,
    )
```

```python
import functools
import math

import jax
import jax.numpy as jnp
import numpy as np
from jax import lax
from jax.experimental import pallas as pl
from jax.experimental.pallas import tpu as pltpu
from jax.sharding import PartitionSpec as P

HEAD_WIDTH = 128
RANK = 16
EPSILON = 1e-05
ROPE_BASE = 500000.0
NX = 4
MASKED = -1e30
LAG_NEAR = 2
LAG_FAR = 4
GROUP = 2
UNROLL = 4
STACK = 2


def clamp(value, low, high):
    return jnp.minimum(jnp.maximum(value, low), high)


def kernel(
    nz,
    nh,
    length_ref,
    prompt_adapter_ref,
    table_ref,
    hidden_any,
    gain_ref,
    wq_ref,
    down_ref,
    up_ref,
    kv_ref,
    freq_ref,
    query_ref,
    out_ref,
    hidden_ref,
    gain,
    normed,
    own_feat,
    ga,
    share,
    share_in,
    slots,
    gw,
    kvb,
    acc,
    start_col,
    slot_col,
    slot_row,
    cosine,
    sine,
    psum,
    scores,
    tops,
    totals,
    stacked,
    hidden_sem,
    recv_a,
    send_a,
    recv_w,
    send_zw,
    send_xw,
    recv_rs,
    send_rs,
    recv_ag,
    send_ag,
    recv_kv,
    send_kf,
    send_kb,
    recv_h,
    send_h,
):
    page_axis = NX * nz
    tokens, width = hidden_ref.shape
    feat = wq_ref.shape[0]
    cols = wq_ref.shape[1]
    heads = cols // HEAD_WIDTH
    own_width = own_feat.shape[1]
    requests = length_ref.shape[0]
    quarter = requests // NX
    pages = kv_ref.shape[0]
    page_rows = kv_ref.shape[1]
    me = lax.axis_index("page")
    head = lax.axis_index("head")
    x = me // nz
    z = me % nz
    z_up = x * nz + (z + 1) % nz
    z_down = x * nz + (z + nz - 1) % nz
    p_up = (me + 1) % page_axis
    p_down = (me + page_axis - 1) % page_axis
    left_x = (x + NX - 1) % NX
    right_x = (x + 1) % NX
    far_x = (x + 2) % NX
    x_up = right_x * nz + z
    x_down = left_x * nz + z
    x_far = far_x * nz + z

    hidden_copy = pltpu.make_async_copy(hidden_any, hidden_ref, hidden_sem)
    hidden_copy.start()

    def send(src, dst, send_sem, recv_sem, page):
        return pltpu.make_async_remote_copy(
            src_ref=src,
            dst_ref=dst,
            send_sem=send_sem,
            recv_sem=recv_sem,
            device_id={"page": page},
            device_id_type=pl.DeviceIdType.MESH,
        )

    barrier = pltpu.get_barrier_semaphore()
    greeted = (z_up, z_down, x_up, x_down, x_far, p_up, p_down)
    for page in greeted:
        pl.semaphore_signal(
            barrier, inc=1, device_id={"page": page}, device_id_type=pl.DeviceIdType.MESH
        )
    for step in range(1, nh):
        pl.semaphore_signal(
            barrier,
            inc=1,
            device_id={"head": (head + step) % nh},
            device_id_type=pl.DeviceIdType.MESH,
        )

    ga[z, 0:RANK, :] = up_ref[...]
    ga[z, RANK : 2 * RANK, :] = down_ref[...]
    gw[z, x] = wq_ref[...]
    for j in range(pages):
        page_block = kv_ref[table_ref[0, j]]
        kvb[0, 0, j * page_rows : (j + 1) * page_rows, :] = page_block[:, :HEAD_WIDTH]
        kvb[0, 1, j * page_rows : (j + 1) * page_rows, :] = page_block[:, HEAD_WIDTH:]
    pl.semaphore_wait(barrier, len(greeted) + nh - 1)

    low = nz * 5 // 16
    high = nz - 1 - low

    def reach(offset):
        return clamp(nz - 1 - (z + 2 * nz - offset) % nz, low, high)

    def kv_forward(offset, half):
        return send(
            kvb.at[offset, half],
            kvb.at[offset + 1, half],
            send_kf.at[offset, half],
            recv_kv.at[offset + 1, half],
            p_up,
        )

    def kv_backward(offset, half):
        return send(
            kvb.at[offset, half],
            kvb.at[offset - 1, half],
            send_kb.at[offset, half],
            recv_kv.at[offset - 1, half],
            p_down,
        )

    def kv_cross(half):
        return send(
            kvb.at[0, half],
            kvb.at[nz, half],
            send_kb.at[0, half],
            recv_kv.at[nz, half],
            x_up,
        )

    def kv_wait(offset, half):
        send(
            kvb.at[0, half],
            kvb.at[offset, half],
            send_kb.at[0, half],
            recv_kv.at[offset, half],
            x_up,
        ).wait_recv()

    def kv_half(j, half):
        reach_up = reach(j)
        back = nz + 1 - j
        reach_back = reach(back)

        @pl.when(j <= reach_up)
        def _():
            kv_wait(j, half)

            @pl.when(j + 1 <= reach_up)
            def _():
                kv_forward(j, half).start()

        @pl.when(back > reach_back)
        def _():
            kv_wait(back, half)

            @pl.when(back - 1 > reach_back)
            def _():
                kv_backward(back, half).start()

    def kv_step(j):
        kv_half(j, 0)
        kv_half(j, 1)

    def position(i):
        distance = (i + 1) // 2
        return jnp.where(i % 2 == 1, (z + nz - distance) % nz, (z + distance) % nz)

    def goes_up(i):
        return ((i % 2 == 1) & ((i + 1) // 2 < nz // 2)) | (i == 0)

    def goes_down(i):
        return (i % 2 == 0) & ((i + 1) // 2 < nz // 2 - 1)

    def down_slot(i):
        return jnp.where(i == 0, nz, i)

    def a_copy(i, page, slot):
        zz = position(i)
        return send(ga.at[zz], ga.at[zz], send_a.at[slot], recv_a.at[zz], page)

    def w_copy(i, page, slot):
        zz = position(i)
        return send(gw.at[zz, x], gw.at[zz, x], send_zw.at[slot], recv_w.at[zz, x], page)

    def forward_z(i):
        @pl.when(goes_up(i))
        def _():
            a_copy(i, z_up, i).start()
            w_copy(i, z_up, i).start()

        @pl.when(goes_down(i))
        def _():
            a_copy(i, z_down, down_slot(i)).start()
            w_copy(i, z_down, down_slot(i)).start()

    def arrive_z(i):
        for copy in (a_copy, w_copy):
            copy(i, z_up, i).wait_recv()

            @pl.when(goes_up(i))
            def _():
                copy(i, z_up, i).start()

            @pl.when(goes_down(i))
            def _():
                copy(i, z_down, down_slot(i)).start()

    def x_copy(i, xx, page, which):
        zz = position(i)
        return send(
            gw.at[zz, xx], gw.at[zz, xx], send_xw.at[which, zz], recv_w.at[zz, xx], page
        )

    def spread_x(i):
        x_copy(i, x, x_up, 0).start()
        x_copy(i, x, x_down, 1).start()

    def near(i):
        x_copy(i, left_x, x_up, 2).wait_recv()

        @pl.when(i % 2 == 0)
        def _():
            x_copy(i, left_x, x_up, 2).start()

        x_copy(i, right_x, x_down, 2).wait_recv()

        @pl.when(i % 2 == 1)
        def _():
            x_copy(i, right_x, x_down, 2).start()

    peers = ((right_x, x_up), (left_x, x_down), (far_x, x_far))

    def share_copy(k):
        xx, page = peers[k]
        return send(
            share.at[pl.ds(xx * quarter, quarter)],
            share_in.at[k],
            send_rs.at[k],
            recv_rs.at[k],
            page,
        )

    def slot_copy(k):
        mine = pl.ds(x * quarter, quarter)
        return send(slots.at[mine], slots.at[mine], send_ag.at[k], recv_ag.at[x], peers[k][1])

    def make_share():
        for r in range(requests):
            wanted = prompt_adapter_ref[r] - x * nz
            block = ga[jnp.minimum(jnp.maximum(wanted, 0), nz - 1)].astype(jnp.float32)
            held = jnp.where((wanted >= 0) & (wanted < nz), 1.0, 0.0)
            share[r] = (block * held).astype(jnp.bfloat16)
        for k in range(3):
            share_copy(k).start()

    def sum_share():
        for k in range(3):
            share_copy(k).wait_recv()
        mine = pl.ds(x * quarter, quarter)
        total = share[mine].astype(jnp.float32)
        for k in range(3):
            total = total + share_in[k].astype(jnp.float32)
        slots[mine] = total.astype(jnp.bfloat16)
        for k in range(3):
            slot_copy(k).start()

    def head_copy(step):
        return pltpu.make_async_remote_copy(
            src_ref=psum.at[0],
            dst_ref=psum.at[step],
            send_sem=send_h.at[step],
            recv_sem=recv_h.at[step],
            device_id={"head": (head + step) % nh},
            device_id_type=pl.DeviceIdType.MESH,
        )

    def use_slots():
        for xx in (left_x, right_x, far_x):
            theirs = pl.ds(xx * quarter, quarter)
            send(
                slots.at[theirs], slots.at[theirs], send_ag.at[0], recv_ag.at[xx], x_up
            ).wait_recv()
        part = lax.dot_general(
            slots[:, RANK : 2 * RANK, :].reshape(requests * RANK, cols),
            own_feat[...],
            (((1,), (1,)), ((), ())),
            preferred_element_type=jnp.float32,
        )
        wanted = slot_row[...]
        wanted = jnp.concatenate([wanted, wanted], axis=0)
        total = jnp.zeros((RANK, tokens), jnp.float32)
        for r in range(requests):
            total += jnp.where(wanted == r, part[r * RANK : (r + 1) * RANK], 0.0)
        psum[0] = total
        for step in range(1, nh):
            head_copy(step).start()

    forward_z(0)
    spread_x(0)
    for half in range(2):

        @pl.when(reach(0) >= 1)
        def _():
            kv_forward(0, half).start()

        kv_cross(half).start()

    def prompts(token):
        start = jnp.zeros(token.shape, jnp.int32)
        slot = jnp.zeros(token.shape, jnp.int32)
        end = jnp.int32(0)
        for r in range(requests):
            begin = end
            end = end + length_ref[r]
            inside = token >= begin
            start = jnp.where(inside, begin, start)
            slot = jnp.where(inside, r, slot)
        return start, slot

    slot_row[...] = prompts(
        me * tokens + lax.broadcasted_iota(jnp.int32, (8, tokens), 1)
    )[1]
    gain[...] = gain_ref[...].astype(jnp.float32)
    acc[...] = jnp.zeros_like(acc)
    hidden_copy.wait()

    rows_step = 32
    norm_steps = tokens // rows_step
    norm_each = (norm_steps + LAG_FAR - 1) // LAG_FAR

    def norm_rows(step, carry):
        rows = pl.ds(pl.multiple_of(step * rows_step, rows_step), rows_step)
        value = hidden_ref[rows, :].astype(jnp.float32)
        scale = lax.rsqrt(jnp.mean(value * value, axis=-1, keepdims=True) + EPSILON)
        lane = lax.broadcasted_iota(jnp.int32, (rows_step, 2 * feat), 1)
        lower = lane < feat
        for pair in range(nz // 2):
            piece = []
            for k in range(NX):
                c = k * nz // 2 + pair
                part = value[:, c * 2 * feat : (c + 1) * 2 * feat] * scale
                piece.append(part * gain[c : c + 1, :])
            for k in range(0, NX, 2):
                even = jnp.where(lower, piece[k], pltpu.roll(piece[k + 1], feat, 1))
                odd = jnp.where(lower, pltpu.roll(piece[k], feat, 1), piece[k + 1])
                normed[2 * pair, rows, k * feat : (k + 2) * feat] = even.astype(jnp.bfloat16)
                normed[2 * pair + 1, rows, k * feat : (k + 2) * feat] = odd.astype(jnp.bfloat16)
        for k in range(own_width // HEAD_WIDTH):
            c = head * (own_width // HEAD_WIDTH) + k
            lanes = pl.ds(pl.multiple_of(c * HEAD_WIDTH, HEAD_WIDTH), HEAD_WIDTH)
            own = hidden_ref[rows, lanes].astype(jnp.float32) * scale * gain[pl.ds(c, 1), :]
            own_feat[rows, k * HEAD_WIDTH : (k + 1) * HEAD_WIDTH] = own.astype(jnp.bfloat16)
        token = me * tokens + step * rows_step + lax.broadcasted_iota(
            jnp.int32, (rows_step, HEAD_WIDTH), 0
        )
        start, slot = prompts(token)
        start_col[rows, :] = start
        slot_col[rows, :] = slot
        return carry

    lane = lax.broadcasted_iota(jnp.int32, (tokens, HEAD_WIDTH), 1)

    def rotation():
        token = me * tokens + lax.broadcasted_iota(jnp.int32, (tokens, HEAD_WIDTH), 0)
        angle = (token - start_col[...]).astype(jnp.float32) * freq_ref[...]
        cosine[...] = jnp.cos(angle)
        turn = jnp.sin(angle)
        sine[...] = jnp.where(lane < HEAD_WIDTH // 2, -turn, turn)

    def at(m, when, body):
        @pl.when(m == when)
        def _():
            body()

    last_z = 3 * (nz // 4) - 1 if nz % 4 == 0 else nz // 2
    gap = 4 if nz >= 16 else 1

    def weights_step(m, carry):
        distance = 2 * (m // 3) + m % 3

        @pl.when((m % 3 != 0) & (distance <= nz // 2))
        def _():
            arrive_z(2 * distance - 1)

            @pl.when(distance < nz // 2)
            def _():
                arrive_z(2 * distance)

        @pl.when((m >= 1) & (m < nz))
        def _():
            spread_x(m)

        @pl.when((m >= LAG_NEAR) & (m < nz + LAG_NEAR))
        def _():
            near(m - LAG_NEAR)

        @pl.when(m < LAG_FAR)
        def _():
            lax.fori_loop(
                m * norm_each,
                jnp.minimum((m + 1) * norm_each, norm_steps),
                norm_rows,
                0,
            )

        at(m, LAG_FAR + 1, rotation)
        at(m, last_z, make_share)
        at(m, last_z + gap, sum_share)
        at(m, last_z + 2 * gap, use_slots)

        @pl.when((m >= 1) & ((m + 1) // 2 <= nz))
        def _():
            kv_half((m + 1) // 2, (m + 1) % 2)

        @pl.when(m >= LAG_FAR)
        def _():
            i = m - LAG_FAR
            zz = position(i)
            x_copy(i, far_x, x_up, 2).wait_recv()
            acc[...] += jnp.dot(
                normed[zz], gw[zz].reshape(NX * feat, cols), preferred_element_type=jnp.float32
            )

        return carry

    lax.fori_loop(0, nz + LAG_FAR, weights_step, 0)
    halves = nz + LAG_FAR - 1
    kv_next = (halves + 1) // 2 + 1
    if halves % 2 == 1 and (halves + 1) // 2 <= nz:
        kv_half(jnp.int32((halves + 1) // 2), 1)

    def service(limit):
        nonlocal kv_next
        while kv_next <= min(limit, nz):
            kv_step(jnp.int32(kv_next))
            kv_next += 1

    first_late = kv_next
    service(first_late)

    for step in range(1, nh):
        head_copy(step).wait_recv()
    shrunk = psum[0]
    for step in range(1, nh):
        shrunk = shrunk + psum[step]
    shrunk = shrunk.astype(jnp.bfloat16).astype(jnp.float32)
    shrunk = jnp.concatenate([shrunk] * (HEAD_WIDTH // RANK), axis=0)
    shrunk = jnp.transpose(shrunk)
    per = HEAD_WIDTH // RANK
    spread = []
    for c in range(requests // per):
        wanted = c * per + lane // RANK
        spread.append(jnp.where(slot_col[...] == wanted, shrunk, 0.0).astype(jnp.bfloat16))
    spread = jnp.concatenate(spread, axis=1)
    acc[...] += jnp.dot(
        spread,
        slots[:, 0:RANK, :].reshape(requests * RANK, cols),
        preferred_element_type=jnp.float32,
    )

    for h in range(heads):
        u = acc[:, h * HEAD_WIDTH : (h + 1) * HEAD_WIDTH]
        turned = u * cosine[...] + pltpu.roll(u, HEAD_WIDTH // 2, 1) * sine[...]
        turned = turned.astype(jnp.bfloat16)
        query_ref[:, h * HEAD_WIDTH : (h + 1) * HEAD_WIDTH] = turned
        stacked[h // STACK, (h % STACK) * tokens : (h % STACK + 1) * tokens, :] = turned

    service(first_late + 1)

    factor = math.log2(math.e) / math.sqrt(HEAD_WIDTH)
    begin = start_col[...] - lane
    row = lax.broadcasted_iota(jnp.int32, (tokens, HEAD_WIDTH), 0)
    pieces = tokens // HEAD_WIDTH
    done = min(first_late + 1, nz)

    def at_hand(offset):
        return offset <= low or offset > nz - low or max(offset, nz + 1 - offset) <= done

    def groups(offsets):
        found = []
        for offset in offsets:
            if found and len(found[-1]) < GROUP and found[-1][-1] + 1 == offset:
                found[-1].append(offset)
            else:
                found.append([offset])
        return found

    early = groups([o for o in range(1, nz + 1) if at_hand(o)])
    late = groups([o for o in range(1, nz + 1) if not at_hand(o)])

    def rows_of(k):
        return slice(k * tokens, (k + 1) * tokens)

    def each(parts, body):
        pairs = [part[0] for part in parts if len(part) == GROUP]

        def one(k, carry):
            offset = jnp.int32(pairs[0])
            for other, start in enumerate(pairs):
                offset = jnp.where(k == other, start, offset)
            body(offset, GROUP)
            return carry

        if pairs:
            lax.fori_loop(0, len(pairs), one, 0, unroll=UNROLL)
        for part in parts:
            if len(part) < GROUP:
                body(part[0], len(part))

    def block_of(offset, count, half):
        return kvb[pl.ds(offset, count), half].reshape(count * tokens, HEAD_WIDTH)

    def score(b, offset, count, own=False):
        block = lax.dot_general(
            stacked[b],
            block_of(offset, count, 0),
            (((1,), (1,)), ((), ())),
            preferred_element_type=jnp.float32,
        )
        for g in range(count):
            base = (me - offset - g) * tokens
            seen = []
            for c in range(pieces):
                visible = begin <= base + c * HEAD_WIDTH
                if own:
                    visible = visible & (lane + c * HEAD_WIDTH <= row)
                seen.append(visible)
            for k in range(STACK):
                top = None if own else tops[b, rows_of(k), :]
                for c in range(pieces):
                    first = (g * pieces + c) * HEAD_WIDTH
                    part = block[rows_of(k), first : first + HEAD_WIDTH]
                    part = jnp.where(seen[c], part, MASKED)
                    scores[
                        offset + g, rows_of(k), c * HEAD_WIDTH : (c + 1) * HEAD_WIDTH
                    ] = part
                    top = part if top is None else jnp.maximum(top, part)
                tops[b, rows_of(k), :] = top

    def level(b):
        for k in range(STACK):
            tops[b, rows_of(k), :] = jnp.broadcast_to(
                jnp.max(tops[b, rows_of(k), :], axis=1, keepdims=True), (tokens, HEAD_WIDTH)
            )

    def mix(b, offset, count, own=False):
        weight = []
        for g in range(count):
            for c in range(pieces):
                part = scores[offset + g, :, c * HEAD_WIDTH : (c + 1) * HEAD_WIDTH]
                weight.append(jnp.exp2((part - tops[b]) * factor).astype(jnp.bfloat16))
        weight = jnp.concatenate(weight, axis=1)
        value = block_of(offset, count, 1)
        value = jnp.concatenate([value, jnp.ones_like(value)], axis=1)
        product = jnp.dot(weight, value, preferred_element_type=jnp.float32)
        totals[b] = product if own else totals[b] + product

    def serve(j):
        @pl.when(j <= nz)
        def _():
            kv_step(jnp.minimum(j, nz))

    def attend_early(b, carry):
        score(b, 0, 1, True)
        each(early, lambda o, n: score(b, o, n))
        level(b)
        serve(done + 1 + 2 * b)
        mix(b, 0, 1, True)
        each(early, lambda o, n: mix(b, o, n))
        serve(done + 2 + 2 * b)
        return carry

    def attend_late(b, carry):
        if late:
            before = tops[b]
            each(late, lambda o, n: score(b, o, n))
            level(b)
            fade = jnp.exp2((before - tops[b]) * factor)
            totals[b] = totals[b] * jnp.concatenate([fade, fade], axis=1)
            each(late, lambda o, n: mix(b, o, n))
        for k in range(STACK):
            total = totals[b, rows_of(k), :]
            h = b * STACK + k
            out_ref[:, pl.ds(pl.multiple_of(h * HEAD_WIDTH, HEAD_WIDTH), HEAD_WIDTH)] = (
                total[:, :HEAD_WIDTH] / total[:, HEAD_WIDTH:]
            ).astype(jnp.bfloat16)
        return carry

    stacks = heads // STACK
    lax.fori_loop(0, stacks, attend_early, 0)
    kv_next = done + 1 + 2 * stacks
    service(nz)
    lax.fori_loop(0, stacks, attend_late, 0)

    def finish(i, carry):
        @pl.when(goes_up(i))
        def _():
            a_copy(i, z_up, i).wait_send()
            w_copy(i, z_up, i).wait_send()

        @pl.when(goes_down(i))
        def _():
            a_copy(i, z_down, down_slot(i)).wait_send()
            w_copy(i, z_down, down_slot(i)).wait_send()

        x_copy(i, x, x_up, 0).wait_send()
        x_copy(i, x, x_down, 1).wait_send()
        x_copy(i, left_x, x_up, 2).wait_send()
        return carry

    lax.fori_loop(0, nz, finish, 0)
    for k in range(3):
        share_copy(k).wait_send()
        slot_copy(k).wait_send()
    for step in range(1, nh):
        head_copy(step).wait_send()

    def kv_finish(j, carry):
        reach_up = reach(j)
        for half in range(2):

            @pl.when(j + 1 <= reach_up)
            def _():
                kv_forward(j, half).wait_send()

            @pl.when(j - 1 > reach_up)
            def _():
                kv_backward(j, half).wait_send()

        return carry

    lax.fori_loop(0, nz + 1, kv_finish, 0)
    for half in range(2):
        kv_cross(half).wait_send()


def relay(first_ref, second_ref, first_out, second_out, sem):
    copies = [
        pltpu.make_async_copy(first_ref, first_out, sem.at[0]),
        pltpu.make_async_copy(second_ref, second_out, sem.at[1]),
    ]
    for copy in copies:
        copy.start()
    for copy in copies:
        copy.wait()


def body(
    nz,
    nh,
    hidden,
    attention_norm_gain,
    wq,
    adapter_down_weight,
    adapter_up_weight,
    key_value_cache,
    logical_page_table,
    lengths,
    prompt_adapter_index,
):
    tokens, width = hidden.shape
    feat, cols = wq.shape
    own_width = adapter_down_weight.shape[0]
    pages = logical_page_table.shape[1]
    requests = lengths.shape[0]
    stacks = cols // HEAD_WIDTH // STACK
    kv = key_value_cache.reshape(pages, tokens // pages, 2 * HEAD_WIDTH)
    half = HEAD_WIDTH // 2
    freq = ROPE_BASE ** (-(np.arange(half, dtype=np.float64) * 2.0 / HEAD_WIDTH))
    freq = np.concatenate([freq, freq])[None, :].astype(np.float32)
    smem = pl.BlockSpec(memory_space=pltpu.SMEM)
    vmem = pl.BlockSpec(memory_space=pltpu.VMEM)
    dma = pltpu.SemaphoreType.DMA
    bf16, f32, i32 = jnp.bfloat16, jnp.float32, jnp.int32
    results = pl.pallas_call(
        functools.partial(kernel, nz, nh),
        name="project_attend",
        out_shape=(
            jax.ShapeDtypeStruct((tokens, cols), bf16),
            jax.ShapeDtypeStruct((tokens, cols), bf16),
        ),
        in_specs=[smem] * 3 + [pl.BlockSpec(memory_space=pl.ANY)] + [vmem] * 6,
        out_specs=(vmem, vmem),
        scratch_shapes=[
            pltpu.VMEM((tokens, width), bf16),
            pltpu.VMEM((width // HEAD_WIDTH, HEAD_WIDTH), f32),
            pltpu.VMEM((nz, tokens, NX * feat), bf16),
            pltpu.VMEM((tokens, own_width), bf16),
            pltpu.VMEM((nz, 2 * RANK, cols), bf16),
            pltpu.VMEM((requests, 2 * RANK, cols), bf16),
            pltpu.VMEM((3, requests // NX, 2 * RANK, cols), bf16),
            pltpu.VMEM((requests, 2 * RANK, cols), bf16),
            pltpu.VMEM((nz, NX, feat, cols), bf16),
            pltpu.VMEM((nz + 1, 2, tokens, HEAD_WIDTH), bf16),
            pltpu.VMEM((tokens, cols), f32),
            pltpu.VMEM((tokens, HEAD_WIDTH), i32),
            pltpu.VMEM((tokens, HEAD_WIDTH), i32),
            pltpu.VMEM((8, tokens), i32),
            pltpu.VMEM((tokens, HEAD_WIDTH), f32),
            pltpu.VMEM((tokens, HEAD_WIDTH), f32),
            pltpu.VMEM((nh, RANK, tokens), f32),
            pltpu.VMEM((nz + 1, STACK * tokens, tokens), f32),
            pltpu.VMEM((stacks, STACK * tokens, HEAD_WIDTH), f32),
            pltpu.VMEM((stacks, STACK * tokens, 2 * HEAD_WIDTH), f32),
            pltpu.VMEM((stacks, STACK * tokens, HEAD_WIDTH), bf16),
            dma(()),
            dma((nz,)),
            dma((nz + 1,)),
            dma((nz, NX)),
            dma((nz + 1,)),
            dma((3, nz)),
            dma((3,)),
            dma((3,)),
            dma((NX,)),
            dma((3,)),
            dma((nz + 1, 2)),
            dma((nz + 1, 2)),
            dma((nz + 1, 2)),
            dma((nh,)),
            dma((nh,)),
        ],
        compiler_params=pltpu.CompilerParams(
            collective_id=0, has_side_effects=True, vmem_limit_bytes=58 << 20
        ),
    )(
        lengths,
        prompt_adapter_index,
        logical_page_table,
        hidden,
        attention_norm_gain.reshape(width // HEAD_WIDTH, HEAD_WIDTH),
        wq,
        adapter_down_weight.T,
        adapter_up_weight,
        kv,
        freq,
    )
    anywhere = pl.BlockSpec(memory_space=pl.ANY)
    return pl.pallas_call(
        relay,
        name="relay",
        out_shape=(
            jax.ShapeDtypeStruct((tokens, cols), bf16),
            jax.ShapeDtypeStruct((tokens, cols), bf16),
        ),
        in_specs=[anywhere] * 2,
        out_specs=(anywhere, anywhere),
        scratch_shapes=[dma((2,))],
    )(*results)


def solution(mesh):
    return jax.shard_map(
        functools.partial(body, mesh.shape["page"] // NX, mesh.shape["head"]),
        mesh=mesh,
        in_specs=(
            P("page", None),
            P(),
            P("page", "head"),
            P("head", "page"),
            P("page", "head"),
            P("page", None, "head"),
            P("page", None),
            P(),
            P(),
        ),
        out_specs=(P("page", "head"), P("page", "head")),
        check_vma=False,
    )
```

```python
import functools
import math

import jax
import jax.numpy as jnp
import numpy as np
from jax import lax
from jax.experimental import pallas as pl
from jax.experimental.pallas import tpu as pltpu
from jax.sharding import PartitionSpec as P

HEAD_WIDTH = 128
RANK = 16
EPSILON = 1e-05
ROPE_BASE = 500000.0
NX = 4
MASKED = -1e30
LAG_NEAR = 2
LAG_FAR = 4
GROUP = 2
UNROLL = 4
STACK = 2


def clamp(value, low, high):
    return jnp.minimum(jnp.maximum(value, low), high)


def kernel(
    nz,
    nh,
    length_ref,
    prompt_adapter_ref,
    table_ref,
    hidden_any,
    gain_ref,
    wq_ref,
    down_ref,
    up_ref,
    kv_ref,
    freq_ref,
    query_ref,
    out_ref,
    hidden_ref,
    gain,
    normed,
    own_feat,
    ga,
    share,
    share_in,
    slots,
    gw,
    kvb,
    acc,
    start_col,
    slot_col,
    slot_row,
    cosine,
    sine,
    psum,
    scores,
    tops,
    totals,
    stacked,
    hidden_sem,
    recv_a,
    send_a,
    recv_w,
    send_zw,
    send_xw,
    recv_rs,
    send_rs,
    recv_ag,
    send_ag,
    recv_kv,
    send_kf,
    send_kb,
    recv_h,
    send_h,
):
    page_axis = NX * nz
    tokens, width = hidden_ref.shape
    feat = wq_ref.shape[0]
    cols = wq_ref.shape[1]
    heads = cols // HEAD_WIDTH
    own_width = own_feat.shape[1]
    requests = length_ref.shape[0]
    quarter = requests // NX
    pages = kv_ref.shape[0]
    page_rows = kv_ref.shape[1]
    me = lax.axis_index("page")
    head = lax.axis_index("head")
    x = me // nz
    z = me % nz
    z_up = x * nz + (z + 1) % nz
    z_down = x * nz + (z + nz - 1) % nz
    p_up = (me + 1) % page_axis
    p_down = (me + page_axis - 1) % page_axis
    left_x = (x + NX - 1) % NX
    right_x = (x + 1) % NX
    far_x = (x + 2) % NX
    x_up = right_x * nz + z
    x_down = left_x * nz + z
    x_far = far_x * nz + z

    hidden_copy = pltpu.make_async_copy(hidden_any, hidden_ref, hidden_sem)
    hidden_copy.start()

    def send(src, dst, send_sem, recv_sem, page):
        return pltpu.make_async_remote_copy(
            src_ref=src,
            dst_ref=dst,
            send_sem=send_sem,
            recv_sem=recv_sem,
            device_id={"page": page},
            device_id_type=pl.DeviceIdType.MESH,
        )

    barrier = pltpu.get_barrier_semaphore()
    greeted = (z_up, z_down, x_up, x_down, x_far, p_up, p_down)
    for page in greeted:
        pl.semaphore_signal(
            barrier, inc=1, device_id={"page": page}, device_id_type=pl.DeviceIdType.MESH
        )
    for step in range(1, nh):
        pl.semaphore_signal(
            barrier,
            inc=1,
            device_id={"head": (head + step) % nh},
            device_id_type=pl.DeviceIdType.MESH,
        )

    ga[z, 0:RANK, :] = up_ref[...]
    ga[z, RANK : 2 * RANK, :] = down_ref[...]
    gw[z, x] = wq_ref[...]
    for j in range(pages):
        page_block = kv_ref[table_ref[0, j]]
        kvb[0, 0, j * page_rows : (j + 1) * page_rows, :] = page_block[:, :HEAD_WIDTH]
        kvb[0, 1, j * page_rows : (j + 1) * page_rows, :] = page_block[:, HEAD_WIDTH:]
    pl.semaphore_wait(barrier, len(greeted) + nh - 1)

    low = nz * 5 // 16
    high = nz - 1 - low

    def reach(offset):
        return clamp(nz - 1 - (z + 2 * nz - offset) % nz, low, high)

    def kv_forward(offset, half):
        return send(
            kvb.at[offset, half],
            kvb.at[offset + 1, half],
            send_kf.at[offset, half],
            recv_kv.at[offset + 1, half],
            p_up,
        )

    def kv_backward(offset, half):
        return send(
            kvb.at[offset, half],
            kvb.at[offset - 1, half],
            send_kb.at[offset, half],
            recv_kv.at[offset - 1, half],
            p_down,
        )

    def kv_cross(half):
        return send(
            kvb.at[0, half],
            kvb.at[nz, half],
            send_kb.at[0, half],
            recv_kv.at[nz, half],
            x_up,
        )

    def kv_wait(offset, half):
        send(
            kvb.at[0, half],
            kvb.at[offset, half],
            send_kb.at[0, half],
            recv_kv.at[offset, half],
            x_up,
        ).wait_recv()

    def kv_half(j, half):
        reach_up = reach(j)
        back = nz + 1 - j
        reach_back = reach(back)

        @pl.when(j <= reach_up)
        def _():
            kv_wait(j, half)

            @pl.when(j + 1 <= reach_up)
            def _():
                kv_forward(j, half).start()

        @pl.when(back > reach_back)
        def _():
            kv_wait(back, half)

            @pl.when(back - 1 > reach_back)
            def _():
                kv_backward(back, half).start()

    def kv_step(j):
        kv_half(j, 0)
        kv_half(j, 1)

    def position(i):
        distance = (i + 1) // 2
        return jnp.where(i % 2 == 1, (z + nz - distance) % nz, (z + distance) % nz)

    def goes_up(i):
        return ((i % 2 == 1) & ((i + 1) // 2 < nz // 2)) | (i == 0)

    def goes_down(i):
        return (i % 2 == 0) & ((i + 1) // 2 < nz // 2 - 1)

    def down_slot(i):
        return jnp.where(i == 0, nz, i)

    def a_copy(i, page, slot):
        zz = position(i)
        return send(ga.at[zz], ga.at[zz], send_a.at[slot], recv_a.at[zz], page)

    def w_copy(i, page, slot):
        zz = position(i)
        return send(gw.at[zz, x], gw.at[zz, x], send_zw.at[slot], recv_w.at[zz, x], page)

    def forward_z(i):
        @pl.when(goes_up(i))
        def _():
            a_copy(i, z_up, i).start()
            w_copy(i, z_up, i).start()

        @pl.when(goes_down(i))
        def _():
            a_copy(i, z_down, down_slot(i)).start()
            w_copy(i, z_down, down_slot(i)).start()

    def arrive_z(i):
        for copy in (a_copy, w_copy):
            copy(i, z_up, i).wait_recv()

            @pl.when(goes_up(i))
            def _():
                copy(i, z_up, i).start()

            @pl.when(goes_down(i))
            def _():
                copy(i, z_down, down_slot(i)).start()

    def x_copy(i, xx, page, which):
        zz = position(i)
        return send(
            gw.at[zz, xx], gw.at[zz, xx], send_xw.at[which, zz], recv_w.at[zz, xx], page
        )

    def spread_x(i):
        x_copy(i, x, x_up, 0).start()
        x_copy(i, x, x_down, 1).start()

    def near(i):
        x_copy(i, left_x, x_up, 2).wait_recv()

        @pl.when(i % 2 == 0)
        def _():
            x_copy(i, left_x, x_up, 2).start()

        x_copy(i, right_x, x_down, 2).wait_recv()

        @pl.when(i % 2 == 1)
        def _():
            x_copy(i, right_x, x_down, 2).start()

    peers = ((right_x, x_up), (left_x, x_down), (far_x, x_far))

    def share_copy(k):
        xx, page = peers[k]
        return send(
            share.at[pl.ds(xx * quarter, quarter)],
            share_in.at[k],
            send_rs.at[k],
            recv_rs.at[k],
            page,
        )

    def slot_copy(k):
        mine = pl.ds(x * quarter, quarter)
        return send(slots.at[mine], slots.at[mine], send_ag.at[k], recv_ag.at[x], peers[k][1])

    def make_share():
        for r in range(requests):
            wanted = prompt_adapter_ref[r] - x * nz
            block = ga[jnp.minimum(jnp.maximum(wanted, 0), nz - 1)].astype(jnp.float32)
            held = jnp.where((wanted >= 0) & (wanted < nz), 1.0, 0.0)
            share[r] = (block * held).astype(jnp.bfloat16)
        for k in range(3):
            share_copy(k).start()

    def sum_share():
        for k in range(3):
            share_copy(k).wait_recv()
        mine = pl.ds(x * quarter, quarter)
        total = share[mine].astype(jnp.float32)
        for k in range(3):
            total = total + share_in[k].astype(jnp.float32)
        slots[mine] = total.astype(jnp.bfloat16)
        for k in range(3):
            slot_copy(k).start()

    def head_copy(step):
        return pltpu.make_async_remote_copy(
            src_ref=psum.at[0],
            dst_ref=psum.at[step],
            send_sem=send_h.at[step],
            recv_sem=recv_h.at[step],
            device_id={"head": (head + step) % nh},
            device_id_type=pl.DeviceIdType.MESH,
        )

    def use_slots():
        for xx in (left_x, right_x, far_x):
            theirs = pl.ds(xx * quarter, quarter)
            send(
                slots.at[theirs], slots.at[theirs], send_ag.at[0], recv_ag.at[xx], x_up
            ).wait_recv()
        part = lax.dot_general(
            slots[:, RANK : 2 * RANK, :].reshape(requests * RANK, cols),
            own_feat[...],
            (((1,), (1,)), ((), ())),
            preferred_element_type=jnp.float32,
        )
        wanted = slot_row[...]
        wanted = jnp.concatenate([wanted, wanted], axis=0)
        total = jnp.zeros((RANK, tokens), jnp.float32)
        for r in range(requests):
            total += jnp.where(wanted == r, part[r * RANK : (r + 1) * RANK], 0.0)
        psum[0] = total
        for step in range(1, nh):
            head_copy(step).start()

    forward_z(0)
    spread_x(0)
    for half in range(2):

        @pl.when(reach(0) >= 1)
        def _():
            kv_forward(0, half).start()

        kv_cross(half).start()

    def prompts(token):
        start = jnp.zeros(token.shape, jnp.int32)
        slot = jnp.zeros(token.shape, jnp.int32)
        end = jnp.int32(0)
        for r in range(requests):
            begin = end
            end = end + length_ref[r]
            inside = token >= begin
            start = jnp.where(inside, begin, start)
            slot = jnp.where(inside, r, slot)
        return start, slot

    slot_row[...] = prompts(
        me * tokens + lax.broadcasted_iota(jnp.int32, (8, tokens), 1)
    )[1]
    gain[...] = gain_ref[...].astype(jnp.float32)
    acc[...] = jnp.zeros_like(acc)
    hidden_copy.wait()

    rows_step = 32
    norm_steps = tokens // rows_step
    norm_each = (norm_steps + LAG_FAR - 1) // LAG_FAR

    def norm_rows(step, carry):
        rows = pl.ds(pl.multiple_of(step * rows_step, rows_step), rows_step)
        value = hidden_ref[rows, :].astype(jnp.float32)
        scale = lax.rsqrt(jnp.mean(value * value, axis=-1, keepdims=True) + EPSILON)
        lane = lax.broadcasted_iota(jnp.int32, (rows_step, 2 * feat), 1)
        lower = lane < feat
        for pair in range(nz // 2):
            piece = []
            for k in range(NX):
                c = k * nz // 2 + pair
                part = value[:, c * 2 * feat : (c + 1) * 2 * feat] * scale
                piece.append(part * gain[c : c + 1, :])
            for k in range(0, NX, 2):
                even = jnp.where(lower, piece[k], pltpu.roll(piece[k + 1], feat, 1))
                odd = jnp.where(lower, pltpu.roll(piece[k], feat, 1), piece[k + 1])
                normed[2 * pair, rows, k * feat : (k + 2) * feat] = even.astype(jnp.bfloat16)
                normed[2 * pair + 1, rows, k * feat : (k + 2) * feat] = odd.astype(jnp.bfloat16)
        for k in range(own_width // HEAD_WIDTH):
            c = head * (own_width // HEAD_WIDTH) + k
            lanes = pl.ds(pl.multiple_of(c * HEAD_WIDTH, HEAD_WIDTH), HEAD_WIDTH)
            own = hidden_ref[rows, lanes].astype(jnp.float32) * scale * gain[pl.ds(c, 1), :]
            own_feat[rows, k * HEAD_WIDTH : (k + 1) * HEAD_WIDTH] = own.astype(jnp.bfloat16)
        token = me * tokens + step * rows_step + lax.broadcasted_iota(
            jnp.int32, (rows_step, HEAD_WIDTH), 0
        )
        start, slot = prompts(token)
        start_col[rows, :] = start
        slot_col[rows, :] = slot
        return carry

    lane = lax.broadcasted_iota(jnp.int32, (tokens, HEAD_WIDTH), 1)

    def rotation():
        token = me * tokens + lax.broadcasted_iota(jnp.int32, (tokens, HEAD_WIDTH), 0)
        angle = (token - start_col[...]).astype(jnp.float32) * freq_ref[...]
        cosine[...] = jnp.cos(angle)
        turn = jnp.sin(angle)
        sine[...] = jnp.where(lane < HEAD_WIDTH // 2, -turn, turn)

    def at(m, when, body):
        @pl.when(m == when)
        def _():
            body()

    last_z = 3 * (nz // 4) - 1 if nz % 4 == 0 else nz // 2
    gap = 4 if nz >= 16 else 1

    def weights_step(m, carry):
        distance = 2 * (m // 3) + m % 3

        @pl.when((m % 3 != 0) & (distance <= nz // 2))
        def _():
            arrive_z(2 * distance - 1)

            @pl.when(distance < nz // 2)
            def _():
                arrive_z(2 * distance)

        @pl.when((m >= 1) & (m < nz))
        def _():
            spread_x(m)

        @pl.when((m >= LAG_NEAR) & (m < nz + LAG_NEAR))
        def _():
            near(m - LAG_NEAR)

        @pl.when(m < LAG_FAR)
        def _():
            lax.fori_loop(
                m * norm_each,
                jnp.minimum((m + 1) * norm_each, norm_steps),
                norm_rows,
                0,
            )

        at(m, LAG_FAR + 1, rotation)
        at(m, last_z, make_share)
        at(m, last_z + gap, sum_share)
        at(m, last_z + 2 * gap, use_slots)

        @pl.when((m >= 1) & ((m + 1) // 2 <= nz))
        def _():
            kv_half((m + 1) // 2, (m + 1) % 2)

        @pl.when(m >= LAG_FAR)
        def _():
            i = m - LAG_FAR
            zz = position(i)
            x_copy(i, far_x, x_up, 2).wait_recv()
            acc[...] += jnp.dot(
                normed[zz], gw[zz].reshape(NX * feat, cols), preferred_element_type=jnp.float32
            )

        return carry

    lax.fori_loop(0, nz + LAG_FAR, weights_step, 0)
    halves = nz + LAG_FAR - 1
    kv_next = (halves + 1) // 2 + 1
    if halves % 2 == 1 and (halves + 1) // 2 <= nz:
        kv_half(jnp.int32((halves + 1) // 2), 1)

    def service(limit):
        nonlocal kv_next
        while kv_next <= min(limit, nz):
            kv_step(jnp.int32(kv_next))
            kv_next += 1

    first_late = kv_next
    service(first_late)

    for step in range(1, nh):
        head_copy(step).wait_recv()
    shrunk = psum[0]
    for step in range(1, nh):
        shrunk = shrunk + psum[step]
    shrunk = shrunk.astype(jnp.bfloat16).astype(jnp.float32)
    shrunk = jnp.concatenate([shrunk] * (HEAD_WIDTH // RANK), axis=0)
    shrunk = jnp.transpose(shrunk)
    per = HEAD_WIDTH // RANK
    spread = []
    for c in range(requests // per):
        wanted = c * per + lane // RANK
        spread.append(jnp.where(slot_col[...] == wanted, shrunk, 0.0).astype(jnp.bfloat16))
    spread = jnp.concatenate(spread, axis=1)
    acc[...] += jnp.dot(
        spread,
        slots[:, 0:RANK, :].reshape(requests * RANK, cols),
        preferred_element_type=jnp.float32,
    )

    for h in range(heads):
        u = acc[:, h * HEAD_WIDTH : (h + 1) * HEAD_WIDTH]
        turned = u * cosine[...] + pltpu.roll(u, HEAD_WIDTH // 2, 1) * sine[...]
        turned = turned.astype(jnp.bfloat16)
        query_ref[:, h * HEAD_WIDTH : (h + 1) * HEAD_WIDTH] = turned
        stacked[h // STACK, (h % STACK) * tokens : (h % STACK + 1) * tokens, :] = turned

    service(first_late + 1)

    factor = math.log2(math.e) / math.sqrt(HEAD_WIDTH)
    begin = start_col[...] - lane
    row = lax.broadcasted_iota(jnp.int32, (tokens, HEAD_WIDTH), 0)
    pieces = tokens // HEAD_WIDTH
    done = min(first_late + 1, nz)

    def at_hand(offset):
        return offset <= low or offset > nz - low or max(offset, nz + 1 - offset) <= done

    def groups(offsets):
        found = []
        for offset in offsets:
            if found and len(found[-1]) < GROUP and found[-1][-1] + 1 == offset:
                found[-1].append(offset)
            else:
                found.append([offset])
        return found

    early = groups([o for o in range(1, nz + 1) if at_hand(o)])
    late = groups([o for o in range(1, nz + 1) if not at_hand(o)])

    def rows_of(k):
        return slice(k * tokens, (k + 1) * tokens)

    def each(parts, body):
        pairs = [part[0] for part in parts if len(part) == GROUP]

        def one(k, carry):
            offset = jnp.int32(pairs[0])
            for other, start in enumerate(pairs):
                offset = jnp.where(k == other, start, offset)
            body(offset, GROUP)
            return carry

        if pairs:
            lax.fori_loop(0, len(pairs), one, 0, unroll=UNROLL)
        for part in parts:
            if len(part) < GROUP:
                body(part[0], len(part))

    def block_of(offset, count, half):
        return kvb[pl.ds(offset, count), half].reshape(count * tokens, HEAD_WIDTH)

    def score(b, offset, count, own=False):
        block = lax.dot_general(
            stacked[b],
            block_of(offset, count, 0),
            (((1,), (1,)), ((), ())),
            preferred_element_type=jnp.float32,
        )
        for g in range(count):
            base = (me - offset - g) * tokens
            seen = []
            for c in range(pieces):
                visible = begin <= base + c * HEAD_WIDTH
                if own:
                    visible = visible & (lane + c * HEAD_WIDTH <= row)
                seen.append(visible)
            for k in range(STACK):
                top = None if own else tops[b, rows_of(k), :]
                for c in range(pieces):
                    first = (g * pieces + c) * HEAD_WIDTH
                    part = block[rows_of(k), first : first + HEAD_WIDTH]
                    part = jnp.where(seen[c], part, MASKED)
                    scores[
                        offset + g, rows_of(k), c * HEAD_WIDTH : (c + 1) * HEAD_WIDTH
                    ] = part
                    top = part if top is None else jnp.maximum(top, part)
                tops[b, rows_of(k), :] = top

    def level(b):
        for k in range(STACK):
            tops[b, rows_of(k), :] = jnp.broadcast_to(
                jnp.max(tops[b, rows_of(k), :], axis=1, keepdims=True), (tokens, HEAD_WIDTH)
            )

    def mix(b, offset, count, own=False):
        weight = []
        for g in range(count):
            for c in range(pieces):
                part = scores[offset + g, :, c * HEAD_WIDTH : (c + 1) * HEAD_WIDTH]
                weight.append(jnp.exp2((part - tops[b]) * factor).astype(jnp.bfloat16))
        weight = jnp.concatenate(weight, axis=1)
        value = block_of(offset, count, 1)
        value = jnp.concatenate([value, jnp.ones_like(value)], axis=1)
        product = jnp.dot(weight, value, preferred_element_type=jnp.float32)
        totals[b] = product if own else totals[b] + product

    def serve(j):
        @pl.when(j <= nz)
        def _():
            kv_step(jnp.minimum(j, nz))

    def attend_early(b, carry):
        score(b, 0, 1, True)
        each(early, lambda o, n: score(b, o, n))
        level(b)
        serve(done + 1 + 2 * b)
        mix(b, 0, 1, True)
        each(early, lambda o, n: mix(b, o, n))
        serve(done + 2 + 2 * b)
        return carry

    def attend_late(b, carry):
        if late:
            before = tops[b]
            each(late, lambda o, n: score(b, o, n))
            level(b)
            fade = jnp.exp2((before - tops[b]) * factor)
            totals[b] = totals[b] * jnp.concatenate([fade, fade], axis=1)
            each(late, lambda o, n: mix(b, o, n))
        for k in range(STACK):
            total = totals[b, rows_of(k), :]
            h = b * STACK + k
            out_ref[:, pl.ds(pl.multiple_of(h * HEAD_WIDTH, HEAD_WIDTH), HEAD_WIDTH)] = (
                total[:, :HEAD_WIDTH] / total[:, HEAD_WIDTH:]
            ).astype(jnp.bfloat16)
        return carry

    stacks = heads // STACK
    lax.fori_loop(0, stacks, attend_early, 0)
    kv_next = done + 1 + 2 * stacks
    service(nz)
    lax.fori_loop(0, stacks, attend_late, 0)

    def finish(i, carry):
        @pl.when(goes_up(i))
        def _():
            a_copy(i, z_up, i).wait_send()
            w_copy(i, z_up, i).wait_send()

        @pl.when(goes_down(i))
        def _():
            a_copy(i, z_down, down_slot(i)).wait_send()
            w_copy(i, z_down, down_slot(i)).wait_send()

        x_copy(i, x, x_up, 0).wait_send()
        x_copy(i, x, x_down, 1).wait_send()
        x_copy(i, left_x, x_up, 2).wait_send()
        return carry

    lax.fori_loop(0, nz, finish, 0)
    for k in range(3):
        share_copy(k).wait_send()
        slot_copy(k).wait_send()
    for step in range(1, nh):
        head_copy(step).wait_send()

    def kv_finish(j, carry):
        reach_up = reach(j)
        for half in range(2):

            @pl.when(j + 1 <= reach_up)
            def _():
                kv_forward(j, half).wait_send()

            @pl.when(j - 1 > reach_up)
            def _():
                kv_backward(j, half).wait_send()

        return carry

    lax.fori_loop(0, nz + 1, kv_finish, 0)
    for half in range(2):
        kv_cross(half).wait_send()


def relay(first_ref, second_ref, first_out, second_out):
    first_out[...] = first_ref[...]
    second_out[...] = second_ref[...]


def body(
    nz,
    nh,
    hidden,
    attention_norm_gain,
    wq,
    adapter_down_weight,
    adapter_up_weight,
    key_value_cache,
    logical_page_table,
    lengths,
    prompt_adapter_index,
):
    tokens, width = hidden.shape
    feat, cols = wq.shape
    own_width = adapter_down_weight.shape[0]
    pages = logical_page_table.shape[1]
    requests = lengths.shape[0]
    stacks = cols // HEAD_WIDTH // STACK
    kv = key_value_cache.reshape(pages, tokens // pages, 2 * HEAD_WIDTH)
    half = HEAD_WIDTH // 2
    freq = ROPE_BASE ** (-(np.arange(half, dtype=np.float64) * 2.0 / HEAD_WIDTH))
    freq = np.concatenate([freq, freq])[None, :].astype(np.float32)
    smem = pl.BlockSpec(memory_space=pltpu.SMEM)
    vmem = pl.BlockSpec(memory_space=pltpu.VMEM)
    dma = pltpu.SemaphoreType.DMA
    bf16, f32, i32 = jnp.bfloat16, jnp.float32, jnp.int32
    results = pl.pallas_call(
        functools.partial(kernel, nz, nh),
        name="project_attend",
        out_shape=(
            jax.ShapeDtypeStruct((tokens, cols), bf16),
            jax.ShapeDtypeStruct((tokens, cols), bf16),
        ),
        in_specs=[smem] * 3 + [pl.BlockSpec(memory_space=pl.ANY)] + [vmem] * 6,
        out_specs=(vmem, vmem),
        scratch_shapes=[
            pltpu.VMEM((tokens, width), bf16),
            pltpu.VMEM((width // HEAD_WIDTH, HEAD_WIDTH), f32),
            pltpu.VMEM((nz, tokens, NX * feat), bf16),
            pltpu.VMEM((tokens, own_width), bf16),
            pltpu.VMEM((nz, 2 * RANK, cols), bf16),
            pltpu.VMEM((requests, 2 * RANK, cols), bf16),
            pltpu.VMEM((3, requests // NX, 2 * RANK, cols), bf16),
            pltpu.VMEM((requests, 2 * RANK, cols), bf16),
            pltpu.VMEM((nz, NX, feat, cols), bf16),
            pltpu.VMEM((nz + 1, 2, tokens, HEAD_WIDTH), bf16),
            pltpu.VMEM((tokens, cols), f32),
            pltpu.VMEM((tokens, HEAD_WIDTH), i32),
            pltpu.VMEM((tokens, HEAD_WIDTH), i32),
            pltpu.VMEM((8, tokens), i32),
            pltpu.VMEM((tokens, HEAD_WIDTH), f32),
            pltpu.VMEM((tokens, HEAD_WIDTH), f32),
            pltpu.VMEM((nh, RANK, tokens), f32),
            pltpu.VMEM((nz + 1, STACK * tokens, tokens), f32),
            pltpu.VMEM((stacks, STACK * tokens, HEAD_WIDTH), f32),
            pltpu.VMEM((stacks, STACK * tokens, 2 * HEAD_WIDTH), f32),
            pltpu.VMEM((stacks, STACK * tokens, HEAD_WIDTH), bf16),
            dma(()),
            dma((nz,)),
            dma((nz + 1,)),
            dma((nz, NX)),
            dma((nz + 1,)),
            dma((3, nz)),
            dma((3,)),
            dma((3,)),
            dma((NX,)),
            dma((3,)),
            dma((nz + 1, 2)),
            dma((nz + 1, 2)),
            dma((nz + 1, 2)),
            dma((nh,)),
            dma((nh,)),
        ],
        compiler_params=pltpu.CompilerParams(
            collective_id=0, has_side_effects=True, vmem_limit_bytes=58 << 20
        ),
    )(
        lengths,
        prompt_adapter_index,
        logical_page_table,
        hidden,
        attention_norm_gain.reshape(width // HEAD_WIDTH, HEAD_WIDTH),
        wq,
        adapter_down_weight.T,
        adapter_up_weight,
        kv,
        freq,
    )
    return pl.pallas_call(
        relay,
        name="relay",
        out_shape=(
            jax.ShapeDtypeStruct((tokens, cols), bf16),
            jax.ShapeDtypeStruct((tokens, cols), bf16),
        ),
        in_specs=[vmem] * 2,
        out_specs=(vmem, vmem),
    )(*results)


def solution(mesh):
    return jax.shard_map(
        functools.partial(body, mesh.shape["page"] // NX, mesh.shape["head"]),
        mesh=mesh,
        in_specs=(
            P("page", None),
            P(),
            P("page", "head"),
            P("head", "page"),
            P("page", "head"),
            P("page", None, "head"),
            P("page", None),
            P(),
            P(),
        ),
        out_specs=(P("page", "head"), P("page", "head")),
        check_vma=False,
    )
```
